1024 devices in a mesh: gx: 8 (over y), gy: 8 (over x), gz: 16 (over z, core).
Axes of the slice: x: 8, y: 8, z: 8, core: 2. Of those that a mesh axis runs over, the one named last changes fastest.
Arguments:
- fields: float32 [5, 256, 128, 1024], P(None, 'gz', 'gx', 'gy'), may hold values from -6 to 6
- tile_writer: int32 [8, 8, 1280, 1], P('gx', 'gy', 'gz'), may hold values from 0 to 63; in each aligned block of 80 rows (0 to 79, 80 to 159, ..., all dimensions but the last counted through in order) at most 2 rows name the same one
Outputs:
- coarse_bands: float32 [5, 32, 16, 128], P(None, None, 'gx', 'gy')
- received: float32 [8192, 32768], P(('gx', 'gy'), 'gz')
The draws below stay inside these ranges and needn't reach their ends.
Inputs may be any that keep to these rules, and one draw needn't show every extreme that they name: `tile_writer`: within each device's 80 entries, no destination is named more than 2 times, a bound that some block reaches.
All inputs are finite; a program needn't handle non-finite values.
Results may differ from the reference program's by a relative error of at most 0.00014.
Values sent between devices are 32-bit elements; how exact they have to be, the bound alone decides.
No kernel may reach another device: no remote copies, remote signals or barrier semaphores. Data moves between devices by JAX's collectives and lax.ppermute only.
A program may use at most 64 MiB of HBM per device.

```python
import math
import jax
import jax.numpy as jnp
import numpy as np
from jax import lax

F = 5
BX = 16
BY = 128
BZ = 16
NX = 128
NY = 1024
NZ = 256
TILES = 80
TILE = 2048
MOST = 2
N_GX = 8
N_GY = 8
N_GZ = 16


def block_scale(rng, extent, split, least, top_value):
    factor_of, own = 1.0, jax.random.fold_in(rng, 6)
    for dim, blocks in split:
        draws = jnp.exp(jax.random.uniform(jax.random.fold_in(own, dim), (blocks,), jnp.float32, least / len(split), top_value / len(split)))
        factor_of = factor_of * jnp.repeat(draws, extent[dim] // blocks).reshape([-1 if axis == dim else 1 for axis in range(len(extent))])
    return factor_of


def routed_block(key, own, number, rows, count, top, reach, lean):
    ranking = jax.random.permutation(key, count)
    crowded, usual = portions_of(count, rows * top, reach, lean, True), portions_of(count, rows * top, reach, lean, False)
    places = jnp.arange(count)

    def named(tallies, turn):
        used = int((tallies > 0).sum())
        fixed = max(1, used // 4)
        passed = fixed + (places - fixed + turn * (used - fixed)) % max(1, count - fixed)
        return jnp.zeros((count,), jnp.int32).at[ranking[jnp.where(places < fixed, places, passed)]].set(jnp.asarray(tallies, jnp.int32))

    tallies = jnp.where(number % 4 == 0, named(crowded, number // 4), named(usual, number - number // 4 - 1))
    mixed = jax.random.permutation(jax.random.fold_in(own, 3), count)
    giver, sink = mixed[0:count // 2 * 2:2], mixed[1:count // 2 * 2:2]
    slack = jnp.minimum(tallies[giver] - 1, reach - tallies[sink]) // 2
    slack = jnp.where((giver == ranking[0]) | (sink == ranking[0]) | (tallies[sink] == 0), 0, jnp.maximum(slack, 0))
    passed = jax.random.randint(jax.random.fold_in(own, 4), (count // 2,), 0, 1 << 20) % (slack + 1)
    tallies = tallies.at[giver].add(-passed).at[sink].add(passed)
    members = jnp.searchsorted(jnp.cumsum(tallies), jnp.arange(rows * top), side="right").astype(jnp.int32)
    grid = members.reshape(top, rows).T
    grid = grid[jax.random.permutation(jax.random.fold_in(own, 1), rows)]
    turn = jax.random.randint(jax.random.fold_in(own, 2), (rows, 1), 0, top)
    return jnp.take_along_axis(grid, (jnp.arange(top)[None, :] + turn) % top, axis=1)


def portions_of(number_of, total, most, lean, full):
    portions = [(1 << 20) // math.isqrt(grade ** lean) + 1 for grade in range(1, number_of + 1)]
    largest = most if full else min(most, max(-(-total // number_of), total * portions[0] // sum(portions)))
    least = 1 if total - largest >= number_of - 1 else 0
    counts, spare = [largest] + [least] * (number_of - 1), total - largest - least * (number_of - 1)
    while spare > 0:
        movable = [i for i in range(1, number_of) if counts[i] < largest] or [i for i in range(1, number_of) if counts[i] < most]
        whole, left = sum([portions[i] for i in movable]), spare
        for i in movable:
            extra = min(most - counts[i], max(1, left * portions[i] // whole), spare)
            counts[i] = counts[i] + extra
            spare = spare - extra
    return np.array(counts)


def bell_draw(stream_key, shape, width, bound, cuts=(), held_as=jnp.bfloat16):
    values = jax.random.normal(stream_key, shape, jnp.float32) * width
    if len(cuts) > 0:
        values = block_scale(stream_key, shape, cuts, -0.22, 0.18) * values
    return jnp.clip(values, min=-bound, max=bound).astype(held_as)


def setup_inputs(seed: int = 0) -> dict:
    arg_keys = jax.random.split(jax.random.key(seed), 3)
    fields = bell_draw(arg_keys[0], (F, NZ, NX, NY), 1.0, 6.0, ((1, 16), (2, 8), (3, 8)), jnp.float32)
    tile_writer_keys = jax.random.split(jax.random.fold_in(arg_keys[1], 1), N_GX * N_GY * (N_GZ * TILES) // TILES)
    tile_writer_turns = jax.random.permutation(jax.random.fold_in(arg_keys[1], 3), N_GX * N_GY * (N_GZ * TILES) // TILES)
    tile_writer = jax.vmap(lambda own, number: routed_block(jax.random.fold_in(arg_keys[1], 2), own, number, TILES, N_GX * N_GY, 1, MOST, 2))(tile_writer_keys, tile_writer_turns).reshape((N_GX, N_GY, N_GZ * TILES, 1))
    return {"fields": fields, "tile_writer": tile_writer}


PREDICT_ONE = -1.586134342059924
UPDATE_ONE = -0.052980118572961
PREDICT_TWO = 0.882911075530934
UPDATE_TWO = 0.443506852043971
LOW_SCALE = 1.0 / 1.149604398860241
HIGH_SCALE = 1.149604398860241


def lifting(values, along):
    length = values.shape[along]
    low_band = lax.slice_in_dim(values, 0, length, 2, along)
    high_band = lax.slice_in_dim(values, 1, length, 2, along)
    high_band = high_band + PREDICT_ONE * (low_band + jnp.roll(low_band, -1, along))
    low_band = low_band + UPDATE_ONE * (jnp.roll(high_band, 1, along) + high_band)
    high_band = high_band + PREDICT_TWO * (low_band + jnp.roll(low_band, -1, along))
    low_band = low_band + UPDATE_TWO * (jnp.roll(high_band, 1, along) + high_band)
    low_band = low_band * LOW_SCALE
    high_band = high_band * HIGH_SCALE
    joined = jnp.stack([low_band, high_band], axis=along + 1)
    return joined.reshape(values.shape)


def one_field(volume):
    results = []
    current = volume
    for depth in range(3):
        result = lifting(lifting(lifting(current, 1), 2), 0)
        results.append(result)
        current = result[::2, ::2, ::2]
    merged = results[2]
    for depth in (1, 0):
        merged = results[depth].at[::2, ::2, ::2].set(merged)
    return merged, current


def reference(fields, tile_writer):
    coefficients, coarse_three = lax.map(one_field, fields)
    level_four = lifting(coarse_three, 1)
    level_five = lifting(level_four[:, ::2], 1)
    coarse_bands = level_four.at[:, ::2].set(level_five)

    groups = N_GX * N_GY
    blocks = coefficients.reshape(F, N_GZ, BZ, N_GX, BX, N_GY, BY)
    blocks = blocks.transpose(3, 5, 1, 0, 2, 4, 6).reshape(groups, N_GZ, TILES, TILE)
    writers = tile_writer.reshape(groups, N_GZ, TILES).astype(jnp.int32)
    onehot = (writers[..., None] == jnp.arange(groups, dtype=jnp.int32)).astype(jnp.int32)
    slots = jnp.sum((jnp.cumsum(onehot, axis=2) - onehot) * onehot, axis=3).astype(jnp.int32)
    source = jnp.broadcast_to(jnp.arange(groups, dtype=jnp.int32)[:, None, None], writers.shape)
    layer = jnp.broadcast_to(jnp.arange(N_GZ, dtype=jnp.int32)[None, :, None], writers.shape)
    inbox = jnp.zeros((groups, groups * MOST, N_GZ, TILE), jnp.float32)
    inbox = inbox.at[writers, source * MOST + slots, layer].set(blocks)
    received = inbox.reshape(groups * groups * MOST, N_GZ * TILE)
    return coarse_bands, received
```

```python
import jax
import jax.numpy as jnp
import ml_dtypes
import numpy as np
from jax import lax
from jax.experimental import pallas as pl
from jax.experimental.pallas import tpu as pltpu
from jax.sharding import PartitionSpec as P

PREDICT_ONE = -1.586134342059924
UPDATE_ONE = -0.052980118572961
PREDICT_TWO = 0.882911075530934
UPDATE_TWO = 0.443506852043971
LOW_SCALE = 1.0 / 1.149604398860241
HIGH_SCALE = 1.149604398860241

F = 5
NB = 16
LN = 128
ROWS = F * NB * NB
TILES = F * NB

LOW_SIDE = (4, 6, 6)
HIGH_SIDE = (3, 5, 7)


def lift_np(values):
    low = values[0::2].copy()
    high = values[1::2].copy()
    high += PREDICT_ONE * (low + np.roll(low, -1, 0))
    low += UPDATE_ONE * (np.roll(high, 1, 0) + high)
    high += PREDICT_TWO * (low + np.roll(low, -1, 0))
    low += UPDATE_TWO * (np.roll(high, 1, 0) + high)
    joined = np.empty_like(values)
    joined[0::2] = low * LOW_SCALE
    joined[1::2] = high * HIGH_SCALE
    return joined


def split(matrix):
    matrix = np.asarray(matrix, np.float32)
    upper = matrix.astype(ml_dtypes.bfloat16)
    lower = (matrix - upper.astype(np.float32)).astype(ml_dtypes.bfloat16)
    return upper, lower


def y_matrices():
    total, start = 8 * LN, 4 * LN
    level = np.eye(total)
    maps = []
    for _ in range(3):
        level = lift_np(level)
        maps.append(level)
        level = level[0::2]
    own = np.zeros((LN, 2 * LN))
    send = np.zeros((32, LN))
    place = np.zeros((32, 2 * LN))
    columns = [lambda j: j, lambda j: LN + 2 * j, lambda j: LN + 4 * j + 1]
    at_low, at_high = 0, 16
    for depth in range(3):
        count = LN >> depth
        first = start >> depth
        block = maps[depth][:, start : start + LN]
        low, high = LOW_SIDE[depth], HIGH_SIDE[depth]
        assert not block[: first - low].any() and not block[first + count + high :].any()
        for j in range(count):
            own[:, columns[depth](j)] = block[first + j]
        for j in range(low):
            send[at_low] = block[first - low + j]
            place[at_low, columns[depth](count - low + j)] = 1
            at_low += 1
        for j in range(high):
            send[at_high] = block[first + count + j]
            place[at_high, columns[depth](j)] = 1
            at_high += 1
    return send, own, place


def lift(values):
    low = {i // 2: v for i, v in values.items() if i % 2 == 0}
    high = {i // 2: v for i, v in values.items() if i % 2 != 0}

    def add(target, source, factor, offsets):
        span = range(min(source) - 1, max(source) + 2)
        result = dict(target)
        for i in span:
            terms = [source[i + o] for o in offsets if i + o in source]
            if terms:
                step = factor * (terms[0] + terms[1] if len(terms) == 2 else terms[0])
                result[i] = result[i] + step if i in result else step
        return result

    high = add(high, low, PREDICT_ONE, (0, 1))
    low = add(low, high, UPDATE_ONE, (-1, 0))
    high = add(high, low, PREDICT_TWO, (0, 1))
    low = add(low, high, UPDATE_TWO, (-1, 0))
    joined = {2 * i: v * LOW_SCALE for i, v in low.items()}
    joined.update({2 * i + 1: v * HIGH_SCALE for i, v in high.items()})
    return joined


def lows(values):
    return {i // 2: v for i, v in values.items() if i % 2 == 0}


def lane_of(shape):
    return lax.broadcasted_iota(jnp.int32, shape, len(shape) - 1)


def dot(a, b, dims):
    return lax.dot_general(a, b, (dims, ((), ())), preferred_element_type=jnp.float32)


def halves(x):
    upper = x.astype(jnp.bfloat16)
    return upper, (x - upper.astype(jnp.float32)).astype(jnp.bfloat16)


def share_y_kernel(fields, send_hi, send_lo, to_low, to_high):
    cells_hi, cells_lo = halves(fields[...])
    dims = ((1,), (1,))
    shares = dot(send_hi[...], cells_hi, dims) + dot(send_hi[...], cells_lo, dims) + dot(send_lo[...], cells_hi, dims)
    to_low[...] = shares[:16]
    to_high[...] = shares[16:]


def fine_shares(values):
    return lift(values)


def coarse_shares(values):
    second = lift(lows(lift(values)))
    third = lift(lows(second))
    return second, third


def send_rows(second, third, second_lane, third_lane, third_far, roll):
    near_low = []
    for i in range(6):
        row = second[i - 6]
        near_low.append(jnp.where(second_lane, row, third[i - 4]) if i < 4 else row)
    near_high = []
    for i in range(5):
        row = second[8 + i]
        near_high.append(jnp.where(second_lane, row, third[4 + i]) if i < 4 else row)
    far_low = jnp.where(third_lane, third[-6], roll(third[-5], 1))
    far_high = jnp.where(third_lane, third[8], jnp.where(third_far, roll(third[10], 2), roll(third[9], 1)))
    return near_low, near_high, far_low, far_high


def share_z_kernel(
    fields, own_hi, own_lo, place, from_low, from_high, fine, coarse, to_low, to_high, to_low_far, to_high_far, work
):
    cells_hi, cells_lo = halves(fields[...])
    dims = ((1,), (0,))
    low_hi, low_lo = halves(from_high[...])
    high_hi, high_lo = halves(from_low[...])
    turned = ((0,), (0,))
    work[...] = (
        dot(cells_hi, own_hi[...], dims)
        + dot(cells_lo, own_hi[...], dims)
        + dot(cells_hi, own_lo[...], dims)
        + dot(low_hi, place[:16], turned)
        + dot(low_lo, place[:16], turned)
        + dot(high_hi, place[16:], turned)
        + dot(high_lo, place[16:], turned)
    )
    shape = (8, LN)
    lane = lane_of(shape)
    second_lane = lane % 2 == 0
    third_lane = lane % 4 == 1
    third_far = lane % 4 == 3

    def roll(x, by):
        return pltpu.roll(x, by, 1)

    for f in range(F):
        for half in (0, 8):
            rows = slice(half, half + 8)
            at = [f * 256 + z * 16 + half for z in range(NB)]
            done = fine_shares({z: work[at[z] : at[z] + 8, :LN] for z in range(NB)})
            for z in range(NB):
                fine[at[z] : at[z] + 8] = done[z]
            for i in range(4):
                to_low[f, i, rows] = done[i - 4]
            for i in range(3):
                to_high[f, i, rows] = done[16 + i]
            second, third = coarse_shares({z: work[at[z] : at[z] + 8, LN:] for z in range(NB)})
            for z in range(8):
                row = jnp.where(second_lane, second[z], third[z // 2]) if z % 2 == 0 else second[z]
                coarse[f * 128 + z * 16 + half : f * 128 + z * 16 + half + 8] = row
            near_low, near_high, far_low, far_high = send_rows(second, third, second_lane, third_lane, third_far, roll)
            for i in range(6):
                to_low[f, 4 + i, rows] = near_low[i]
            for i in range(5):
                to_high[f, 3 + i, rows] = near_high[i]
            to_low_far[f, rows] = far_low
            to_high_far[f, rows] = far_high


def add_coarse(base, near_low, near_high, far_low, far_high, second_lane, third_lane, roll):
    zero = jnp.zeros_like(base[0])
    rows = list(base)
    for i in range(6):
        rows[2 + i] = rows[2 + i] + jnp.where(second_lane, near_low[i], zero)
    for i in range(5):
        rows[i] = rows[i] + jnp.where(second_lane, near_high[i], zero)
    third = [near_low[r] + near_high[r] for r in range(4)]
    third[2] = third[2] + far_low
    third[3] = third[3] + roll(far_low, LN - 1)
    third[0] = third[0] + far_high
    third[1] = third[1] + roll(far_high, LN - 1)
    third[2] = third[2] + roll(far_high, LN - 2)
    for r in range(4):
        rows[2 * r] = rows[2 * r] + jnp.where(third_lane, third[r], zero)
    return rows


def share_x_kernel(
    fine, coarse, from_high, from_low, from_high_far, from_low_far,
    own_fine, own_coarse, to_low, to_high, to_low_far, to_high_far, work, work_coarse,
):
    shape = (8, LN)
    lane = lane_of(shape)
    second_lane = lane % 2 == 0
    third_lane = lane % 4 == 1
    third_far = lane % 4 == 3

    def roll(x, by):
        return pltpu.roll(x, by, 1)

    for f in range(F):
        at = f * 256
        work[at : at + 48] = fine[at : at + 48] + from_low[f, :3].reshape(48, LN)
        work[at + 48 : at + 192] = fine[at + 48 : at + 192]
        work[at + 192 : at + 256] = fine[at + 192 : at + 256] + from_high[f, :4].reshape(64, LN)
        for half in (0, 8):
            rows = slice(half, half + 8)
            at = [f * 128 + z * 16 + half for z in range(8)]
            added = add_coarse(
                [coarse[at[z] : at[z] + 8] for z in range(8)],
                [from_high[f, 4 + i, rows] for i in range(6)],
                [from_low[f, 3 + i, rows] for i in range(5)],
                from_high_far[f, rows],
                from_low_far[f, rows],
                second_lane,
                third_lane,
                roll,
            )
            for z in range(8):
                work_coarse[at[z] : at[z] + 8] = added[z]
    for g in range(10):
        rows = slice(g * 8, g * 8 + 8)
        done = fine_shares({x: work[pl.ds(g * 128 + x, 8, stride=16), :] for x in range(NB)})
        for x in range(NB):
            own_fine[x, rows] = done[x]
        for i in range(4):
            to_low[i * 80 + g * 8 : i * 80 + g * 8 + 8] = done[i - 4]
        for i in range(3):
            to_high[i * 80 + g * 8 : i * 80 + g * 8 + 8] = done[16 + i]
    for g in range(5):
        rows = slice(g * 8, g * 8 + 8)
        second, third = coarse_shares({x: work_coarse[pl.ds(g * 128 + x, 8, stride=16), :] for x in range(NB)})
        for x in range(8):
            own_coarse[x, rows] = jnp.where(second_lane, second[x], third[x // 2]) if x % 2 == 0 else second[x]
        near_low, near_high, far_low, far_high = send_rows(second, third, second_lane, third_lane, third_far, roll)
        for i in range(6):
            to_low[320 + i * 40 + g * 8 : 320 + i * 40 + g * 8 + 8] = near_low[i]
        for i in range(5):
            to_high[240 + i * 40 + g * 8 : 240 + i * 40 + g * 8 + 8] = near_high[i]
        to_low_far[rows] = far_low
        to_high_far[rows] = far_high


def route_kernel(
    writers, fine, coarse, from_high, from_low, from_high_far, from_low_far, pick,
    outbox, low_band, tiles, spread, counts,
):
    shape = (8, LN)
    lane = lane_of(shape)
    second_lane = lane % 2 == 0
    third_lane = lane % 4 == 1
    replaced = (lane % 4 == 0) & (lax.broadcasted_iota(jnp.int32, shape, 0) % 2 == 0)

    def roll(x, by):
        return pltpu.roll(x, by, 1)

    outbox[...] = jnp.zeros_like(outbox)
    for g in range(5):
        rows = slice(g * 8, g * 8 + 8)
        added = add_coarse(
            [coarse[x, rows] for x in range(8)],
            [from_high[320 + i * 40 + g * 8 : 320 + i * 40 + g * 8 + 8] for i in range(6)],
            [from_low[240 + i * 40 + g * 8 : 240 + i * 40 + g * 8 + 8] for i in range(5)],
            from_high_far[rows],
            from_low_far[rows],
            second_lane,
            third_lane,
            roll,
        )
        for i, x in ((0, 0), (1, 4)):
            upper, lower = halves(added[x])
            rest = (added[x] - upper.astype(jnp.float32) - lower.astype(jnp.float32)).astype(jnp.bfloat16)
            dims = ((1,), (0,))
            low_band[i, rows] = dot(upper, pick[...], dims) + dot(lower, pick[...], dims) + dot(rest, pick[...], dims)
        for x in range(8):
            row = added[x]
            if x % 2 == 0:
                row = jnp.where(replaced, roll(row, LN - 1), row)
            spread[pl.ds(x * 80 + g * 16, 8, stride=2), :] = row
            spread[pl.ds(x * 80 + g * 16 + 1, 8, stride=2), :] = row
    merged = (lane % 2 == 0) & (lax.broadcasted_iota(jnp.int32, shape, 0) % 2 == 0)
    for g in range(10):
        rows = slice(g * 8, g * 8 + 8)
        for x in range(NB):
            row = fine[x, rows]
            if x < 3:
                row = row + from_low[x * 80 + g * 8 : x * 80 + g * 8 + 8]
            if x >= 12:
                i = x - 12
                row = row + from_high[i * 80 + g * 8 : i * 80 + g * 8 + 8]
            if x % 2 == 0:
                row = jnp.where(merged, spread[x // 2 * 80 + g * 8 : x // 2 * 80 + g * 8 + 8], row)
            tiles[pl.ds(g * 128 + x, 8, stride=16), :] = row

    def clear(i, carry):
        counts[i] = 0
        return carry

    lax.fori_loop(0, 64, clear, 0)

    def send(t, carry):
        writer = writers[t]
        slot = counts[writer]
        counts[writer] = slot + 1
        to = pl.multiple_of((writer * 2 + slot) * 16, 16)
        outbox[pl.ds(to, 16), :] = tiles[pl.ds(pl.multiple_of(t * 16, 16), 16), :]
        return carry

    lax.fori_loop(0, TILES, send, 0)


VM = pl.BlockSpec(memory_space=pltpu.VMEM)
SM = pl.BlockSpec(memory_space=pltpu.SMEM)


def f32(*shape):
    return jax.ShapeDtypeStruct(shape, jnp.float32)


def call(kernel, outs, ins, scratch=(), specs=None, flops=1 << 20):
    moved = sum(4 * int(np.prod(a.shape)) for a in list(outs) + list(ins))
    return pl.pallas_call(
        kernel,
        out_shape=list(outs),
        in_specs=specs or [VM] * len(ins),
        out_specs=[VM] * len(outs),
        scratch_shapes=list(scratch),
        compiler_params=pltpu.CompilerParams(vmem_limit_bytes=32 << 20),
        cost_estimate=pl.CostEstimate(flops=flops, bytes_accessed=moved, transcendentals=0),
    )(*ins)


def shift(array, axis, by):
    count = lax.axis_size(axis)
    return lax.ppermute(array, axis, [(i, (i + by) % count) for i in range(count)])


def coarse_matrix(length):
    level_four = lift_np(np.eye(length))
    level_five = lift_np(level_four[0::2])
    level_four[0::2] = level_five
    return level_four.astype(np.float32)


def body(fields, tile_writer):
    send, own, place = y_matrices()
    send_hi, send_lo = (jnp.asarray(m) for m in split(send))
    own_hi, own_lo = (jnp.asarray(m) for m in split(own))
    place = jnp.asarray(place.astype(ml_dtypes.bfloat16))
    pick = np.zeros((LN, 16), ml_dtypes.bfloat16)
    for j in range(16):
        pick[8 * j + 1, j] = 1
    cells = fields.reshape(ROWS, LN)

    to_low, to_high = call(share_y_kernel, [f32(16, ROWS)] * 2, [cells, send_hi, send_lo])
    from_high = shift(to_low, "gy", -1)
    from_low = shift(to_high, "gy", 1)

    fine, coarse, to_low, to_high, to_low_far, to_high_far = call(
        share_z_kernel,
        [f32(ROWS, LN), f32(ROWS // 2, LN), f32(F, 10, 16, LN), f32(F, 8, 16, LN), f32(F, 16, LN), f32(F, 16, LN)],
        [cells, own_hi, own_lo, place, from_low, from_high],
        [pltpu.VMEM((ROWS, 2 * LN), jnp.float32)],
    )
    from_high = shift(to_low, "gz", -1)
    from_low = shift(to_high, "gz", 1)
    from_high_far = shift(to_low_far, "gz", -2)
    from_low_far = shift(to_high_far, "gz", 2)

    fine, coarse, to_low, to_high, to_low_far, to_high_far = call(
        share_x_kernel,
        [f32(16, 80, LN), f32(8, 40, LN), f32(560, LN), f32(440, LN), f32(40, LN), f32(40, LN)],
        [fine, coarse, from_high, from_low, from_high_far, from_low_far],
        [pltpu.VMEM((ROWS, LN), jnp.float32), pltpu.VMEM((ROWS // 2, LN), jnp.float32)],
    )
    from_high = shift(to_low, "gx", -1)
    from_low = shift(to_high, "gx", 1)
    from_high_far = shift(to_low_far, "gx", -2)
    from_low_far = shift(to_high_far, "gx", 2)

    outbox, low_band = call(
        route_kernel,
        [f32(2048, LN), f32(2, 40, 16)],
        [tile_writer.reshape(TILES), fine, coarse, from_high, from_low, from_high_far, from_low_far, jnp.asarray(pick)],
        [pltpu.VMEM((ROWS, LN), jnp.float32), pltpu.VMEM((640, LN), jnp.float32), pltpu.SMEM((64,), jnp.int32)],
        [SM] + [VM] * 7,
    )
    inbox = lax.all_to_all(outbox.reshape(64, 32, LN), ("gx", "gy"), split_axis=0, concat_axis=0, tiled=True)

    band = low_band.reshape(2, F, 8, 16)[:, :, ::4].transpose(2, 1, 0, 3).reshape(2, F * 32)
    band = lax.all_gather(band, "gz", axis=0, tiled=True)
    turn = jnp.asarray(coarse_matrix(band.shape[0]))
    bands = jnp.dot(turn, band, precision=lax.Precision.HIGHEST)
    bands = bands.reshape(-1, F, 2, 16).transpose(1, 0, 2, 3)
    return (bands, inbox.reshape(128, 2048))


def solution(mesh):
    return jax.shard_map(
        body,
        mesh=mesh,
        in_specs=(P(None, "gz", "gx", "gy"), P("gx", "gy", "gz", None)),
        out_specs=(P(None, None, "gx", "gy"), P(("gx", "gy"), "gz")),
        check_vma=False,
    )
```

```python
import jax
import jax.numpy as jnp
import ml_dtypes
import numpy as np
from jax import lax
from jax.experimental import pallas as pl
from jax.experimental.pallas import tpu as pltpu
from jax.sharding import PartitionSpec as P

PREDICT_ONE = -1.586134342059924
UPDATE_ONE = -0.052980118572961
PREDICT_TWO = 0.882911075530934
UPDATE_TWO = 0.443506852043971
LOW_SCALE = 1.0 / 1.149604398860241
HIGH_SCALE = 1.149604398860241

F = 5
NB = 16
LN = 128
ROWS = F * NB * NB
TILES = F * NB

LOW_SIDE = (4, 6, 6)
HIGH_SIDE = (3, 5, 7)


def lift_np(values):
    low = values[0::2].copy()
    high = values[1::2].copy()
    high += PREDICT_ONE * (low + np.roll(low, -1, 0))
    low += UPDATE_ONE * (np.roll(high, 1, 0) + high)
    high += PREDICT_TWO * (low + np.roll(low, -1, 0))
    low += UPDATE_TWO * (np.roll(high, 1, 0) + high)
    joined = np.empty_like(values)
    joined[0::2] = low * LOW_SCALE
    joined[1::2] = high * HIGH_SCALE
    return joined


def split(matrix):
    matrix = np.asarray(matrix, np.float32)
    upper = matrix.astype(ml_dtypes.bfloat16)
    lower = (matrix - upper.astype(np.float32)).astype(ml_dtypes.bfloat16)
    return upper, lower


def y_matrices():
    total, start = 8 * LN, 4 * LN
    level = np.eye(total)
    maps = []
    for _ in range(3):
        level = lift_np(level)
        maps.append(level)
        level = level[0::2]
    own = np.zeros((LN, 2 * LN))
    send = np.zeros((32, LN))
    place = np.zeros((32, 2 * LN))
    columns = [lambda j: j, lambda j: LN + 2 * j, lambda j: LN + 4 * j + 1]
    at_low, at_high = 0, 16
    for depth in range(3):
        count = LN >> depth
        first = start >> depth
        block = maps[depth][:, start : start + LN]
        low, high = LOW_SIDE[depth], HIGH_SIDE[depth]
        assert not block[: first - low].any() and not block[first + count + high :].any()
        for j in range(count):
            own[:, columns[depth](j)] = block[first + j]
        for j in range(low):
            send[at_low] = block[first - low + j]
            place[at_low, columns[depth](count - low + j)] = 1
            at_low += 1
        for j in range(high):
            send[at_high] = block[first + count + j]
            place[at_high, columns[depth](j)] = 1
            at_high += 1
    return send, own, place


def lift(values):
    low = {i // 2: v for i, v in values.items() if i % 2 == 0}
    high = {i // 2: v for i, v in values.items() if i % 2 != 0}

    def add(target, source, factor, offsets):
        span = range(min(source) - 1, max(source) + 2)
        result = dict(target)
        for i in span:
            terms = [source[i + o] for o in offsets if i + o in source]
            if terms:
                step = factor * (terms[0] + terms[1] if len(terms) == 2 else terms[0])
                result[i] = result[i] + step if i in result else step
        return result

    high = add(high, low, PREDICT_ONE, (0, 1))
    low = add(low, high, UPDATE_ONE, (-1, 0))
    high = add(high, low, PREDICT_TWO, (0, 1))
    low = add(low, high, UPDATE_TWO, (-1, 0))
    joined = {2 * i: v * LOW_SCALE for i, v in low.items()}
    joined.update({2 * i + 1: v * HIGH_SCALE for i, v in high.items()})
    return joined


def lows(values):
    return {i // 2: v for i, v in values.items() if i % 2 == 0}


def dot(a, b, dims):
    return lax.dot_general(a, b, (dims, ((), ())), preferred_element_type=jnp.float32)


def halves(x):
    upper = x.astype(jnp.bfloat16)
    return upper, (x - upper.astype(jnp.float32)).astype(jnp.bfloat16)


def share_y_kernel(fields, send, to_low, to_high, cells, matrix, sems):
    copies = [
        pltpu.make_async_copy(fields, cells, sems.at[0]),
        pltpu.make_async_copy(send, matrix, sems.at[1]),
    ]
    for copy in copies:
        copy.start()
    for copy in copies:
        copy.wait()
    cells_hi, cells_lo = halves(cells[...])
    send_hi, send_lo = matrix[:32], matrix[32:]
    dims = ((1,), (1,))
    shares = dot(send_hi, cells_hi, dims) + dot(send_hi, cells_lo, dims) + dot(send_lo, cells_hi, dims)
    to_low[...] = shares[:16]
    to_high[...] = shares[16:]


def slots_kernel(writers, targets, counts):
    for i in range(64):
        counts[i] = 0
    for t in range(TILES):
        writer = writers[t]
        slot = counts[writer]
        counts[writer] = slot + 1
        targets[t] = writer * 2 + slot


def fine_shares(values):
    return lift(values)


def coarse_shares(values):
    second = lift(lows(lift(values)))
    third = lift(lows(second))
    return second, third


class Lanes:
    def __init__(self):
        self.lane = lax.broadcasted_iota(jnp.int32, (8, LN), 1)
        self.second = self.lane % 2 == 0
        self.third = self.lane % 4 == 1
        self.ahead = [self.lane % 4 == (1 + i) % 4 for i in range(4)]

    @staticmethod
    def roll(x, by):
        return pltpu.roll(x, by % LN, 1) if by % LN else x

    def pack_second(self, rows):
        packed = []
        for i in range(0, len(rows), 2):
            odd = self.roll(rows[i + 1], 1) if i + 1 < len(rows) else rows[i]
            packed.append(jnp.where(self.second, rows[i], odd))
        return packed

    def pack_third(self, rows):
        packed = rows[0]
        for i in range(1, len(rows)):
            packed = jnp.where(self.ahead[i], self.roll(rows[i], i), packed)
        return packed


def send_rows(second, third, lanes):
    near_low = lanes.pack_second([second[i - 6] for i in range(6)]) + [lanes.pack_third([third[i - 4] for i in range(4)])]
    near_high = lanes.pack_second([second[8 + i] for i in range(5)]) + [lanes.pack_third([third[4 + i] for i in range(4)])]
    return near_low, near_high, lanes.pack_third([third[-6], third[-5]]), lanes.pack_third([third[8], third[9], third[10]])


def share_z_kernel(
    fields, maps, from_low, from_high, fine, coarse, to_low, to_high, to_low_far, to_high_far, work
):
    cells_hi, cells_lo = halves(fields[...])
    dims = ((1,), (0,))
    low_hi, low_lo = halves(from_high[...])
    high_hi, high_lo = halves(from_low[...])
    turned = ((0,), (0,))
    own_hi, own_lo, place_low, place_high = maps[:128], maps[128:256], maps[256:272], maps[272:]
    work[...] = (
        dot(cells_hi, own_hi, dims)
        + dot(cells_lo, own_hi, dims)
        + dot(cells_hi, own_lo, dims)
        + dot(low_hi, place_low, turned)
        + dot(low_lo, place_low, turned)
        + dot(high_hi, place_high, turned)
        + dot(high_lo, place_high, turned)
    )
    lanes = Lanes()
    for f in range(F):
        for half in (0, 8):
            rows = slice(half, half + 8)
            at = [f * 256 + z * 16 + half for z in range(NB)]
            done = fine_shares({z: work[at[z] : at[z] + 8, :LN] for z in range(NB)})
            for z in range(NB):
                fine[at[z] : at[z] + 8] = done[z]
            for i in range(4):
                to_low[f, i, rows] = done[i - 4]
            for i in range(3):
                to_high[f, i, rows] = done[16 + i]
            second, third = coarse_shares({z: work[at[z] : at[z] + 8, LN:] for z in range(NB)})
            for z in range(8):
                row = jnp.where(lanes.second, second[z], third[z // 2]) if z % 2 == 0 else second[z]
                coarse[f * 128 + z * 16 + half : f * 128 + z * 16 + half + 8] = row
            near_low, near_high, far_low, far_high = send_rows(second, third, lanes)
            for i in range(4):
                to_low[f, 4 + i, rows] = near_low[i]
                to_high[f, 3 + i, rows] = near_high[i]
            to_low_far[f, rows] = far_low
            to_high_far[f, rows] = far_high


def add_coarse(base, near_low, near_high, far_low, far_high, lanes):
    zero = jnp.zeros_like(base[0])
    extra = [zero] * 8
    for i in range(6):
        extra[2 + i] = extra[2 + i] + lanes.roll(near_low[i // 2], -(i % 2))
    for i in range(5):
        extra[i] = extra[i] + lanes.roll(near_high[i // 2], -(i % 2))
    near = near_low[3] + near_high[3]
    near = near + jnp.where(lanes.ahead[3], zero, far_high)
    third = [lanes.roll(near, -r) for r in range(4)]
    third[2] = third[2] + far_low
    third[3] = third[3] + lanes.roll(far_low, -1)
    rows = []
    for i in range(8):
        other = jnp.where(lanes.third, third[i // 2], zero) if i % 2 == 0 else zero
        rows.append(base[i] + jnp.where(lanes.second, extra[i], other))
    return rows


def share_x_kernel(
    fine, coarse, from_high, from_low, from_high_far, from_low_far,
    own_fine, own_coarse, to_low, to_high, to_low_far, to_high_far, work, work_coarse,
):
    lanes = Lanes()
    for f in range(F):
        at = f * 256
        work[at : at + 48] = fine[at : at + 48] + from_low[f, :3].reshape(48, LN)
        work[at + 48 : at + 192] = fine[at + 48 : at + 192]
        work[at + 192 : at + 256] = fine[at + 192 : at + 256] + from_high[f, :4].reshape(64, LN)
        for half in (0, 8):
            rows = slice(half, half + 8)
            at = [f * 128 + z * 16 + half for z in range(8)]
            added = add_coarse(
                [coarse[at[z] : at[z] + 8] for z in range(8)],
                [from_high[f, 4 + i, rows] for i in range(4)],
                [from_low[f, 3 + i, rows] for i in range(4)],
                from_high_far[f, rows],
                from_low_far[f, rows],
                lanes,
            )
            for z in range(8):
                work_coarse[at[z] : at[z] + 8] = added[z]
    for g in range(10):
        rows = slice(g * 8, g * 8 + 8)
        done = fine_shares({x: work[pl.ds(g * 128 + x, 8, stride=16), :] for x in range(NB)})
        for x in range(NB):
            own_fine[x, rows] = done[x]
        for i in range(4):
            to_low[i * 80 + g * 8 : i * 80 + g * 8 + 8] = done[i - 4]
        for i in range(3):
            to_high[i * 80 + g * 8 : i * 80 + g * 8 + 8] = done[16 + i]
    for g in range(5):
        rows = slice(g * 8, g * 8 + 8)
        second, third = coarse_shares({x: work_coarse[pl.ds(g * 128 + x, 8, stride=16), :] for x in range(NB)})
        for x in range(8):
            own_coarse[x, rows] = jnp.where(lanes.second, second[x], third[x // 2]) if x % 2 == 0 else second[x]
        near_low, near_high, far_low, far_high = send_rows(second, third, lanes)
        for i in range(4):
            to_low[320 + i * 40 + g * 8 : 320 + i * 40 + g * 8 + 8] = near_low[i]
            to_high[240 + i * 40 + g * 8 : 240 + i * 40 + g * 8 + 8] = near_high[i]
        to_low_far[rows] = far_low
        to_high_far[rows] = far_high


def route_kernel(
    targets, fine, coarse, from_high, from_low, from_high_far, from_low_far, outbox, low_band, tiles, spread
):
    shape = (8, LN)
    lanes = Lanes()
    lane = lanes.lane
    even_row = lax.broadcasted_iota(jnp.int32, shape, 0) % 2 == 0
    replaced = (lane % 4 == 0) & even_row
    merged = lanes.second & even_row
    picked = (LN, 16)
    pick = lax.broadcasted_iota(jnp.int32, picked, 0) == 8 * lax.broadcasted_iota(jnp.int32, picked, 1) + 1
    pick = jnp.where(pick, jnp.ones(picked, jnp.float32), jnp.zeros(picked, jnp.float32)).astype(jnp.bfloat16)
    outbox[...] = jnp.zeros_like(outbox)
    for g in range(5):
        rows = slice(g * 8, g * 8 + 8)
        added = add_coarse(
            [coarse[x, rows] for x in range(8)],
            [from_high[320 + i * 40 + g * 8 : 320 + i * 40 + g * 8 + 8] for i in range(4)],
            [from_low[240 + i * 40 + g * 8 : 240 + i * 40 + g * 8 + 8] for i in range(4)],
            from_high_far[rows],
            from_low_far[rows],
            lanes,
        )
        for i, x in ((0, 0), (1, 4)):
            upper, lower = halves(added[x])
            rest = (added[x] - upper.astype(jnp.float32) - lower.astype(jnp.float32)).astype(jnp.bfloat16)
            dims = ((1,), (0,))
            low_band[i, rows] = dot(upper, pick, dims) + dot(lower, pick, dims) + dot(rest, pick, dims)
        for x in range(8):
            row = added[x]
            if x % 2 == 0:
                row = jnp.where(replaced, lanes.roll(row, -1), row)
            spread[pl.ds(x * 80 + g * 16, 8, stride=2), :] = row
            spread[pl.ds(x * 80 + g * 16 + 1, 8, stride=2), :] = row
    for g in range(10):
        rows = slice(g * 8, g * 8 + 8)
        for x in range(NB):
            row = fine[x, rows]
            if x < 3:
                row = row + from_low[x * 80 + g * 8 : x * 80 + g * 8 + 8]
            if x >= 12:
                i = x - 12
                row = row + from_high[i * 80 + g * 8 : i * 80 + g * 8 + 8]
            if x % 2 == 0:
                row = jnp.where(merged, spread[x // 2 * 80 + g * 8 : x // 2 * 80 + g * 8 + 8], row)
            tiles[pl.ds(g * 128 + x, 8, stride=16), :] = row

    for t in range(TILES):
        to = pl.multiple_of(targets[t] * 16, 16)
        outbox[pl.ds(to, 16), :] = tiles[t * 16 : t * 16 + 16]


VM = pl.BlockSpec(memory_space=pltpu.VMEM)
SM = pl.BlockSpec(memory_space=pltpu.SMEM)
HB = pl.BlockSpec(memory_space=pltpu.HBM)


def f32(*shape):
    return jax.ShapeDtypeStruct(shape, jnp.float32)


def call(kernel, outs, ins, scratch=(), specs=None, out_specs=None, flops=1 << 20, grant=32 << 20):
    moved = sum(4 * int(np.prod(a.shape)) for a in list(outs) + list(ins))
    return pl.pallas_call(
        kernel,
        out_shape=list(outs),
        in_specs=specs or [VM] * len(ins),
        out_specs=out_specs or [VM] * len(outs),
        scratch_shapes=list(scratch),
        compiler_params=pltpu.CompilerParams(vmem_limit_bytes=grant),
        cost_estimate=pl.CostEstimate(flops=flops, bytes_accessed=moved, transcendentals=0),
    )(*ins)


def shift(array, axis, by):
    count = lax.axis_size(axis)
    return lax.ppermute(array, axis, [(i, (i + by) % count) for i in range(count)])


def coarse_matrix(length):
    level_four = lift_np(np.eye(length))
    level_five = lift_np(level_four[0::2])
    level_four[0::2] = level_five
    return level_four.astype(np.float32)


def body(fields, tile_writer):
    send, own, place = y_matrices()
    send = jnp.asarray(np.concatenate(split(send)))
    maps = jnp.asarray(np.concatenate([*split(own), place.astype(ml_dtypes.bfloat16)]))
    cells = fields.reshape(ROWS, LN)

    to_low, to_high = call(
        share_y_kernel,
        [f32(16, ROWS)] * 2,
        [cells, send],
        [pltpu.VMEM((ROWS, LN), jnp.float32), pltpu.VMEM((64, LN), jnp.bfloat16), pltpu.SemaphoreType.DMA((2,))],
        [HB, HB],
        grant=60 << 20,
    )
    from_high = shift(to_low, "gy", -1)
    from_low = shift(to_high, "gy", 1)

    (targets,) = call(
        slots_kernel,
        [jax.ShapeDtypeStruct((TILES,), jnp.int32)],
        [tile_writer.reshape(TILES)],
        [pltpu.SMEM((64,), jnp.int32)],
        [SM],
        [SM],
        flops=1 << 30,
    )
    fine, coarse, to_low, to_high, to_low_far, to_high_far = call(
        share_z_kernel,
        [f32(ROWS, LN), f32(ROWS // 2, LN), f32(F, 8, 16, LN), f32(F, 7, 16, LN), f32(F, 16, LN), f32(F, 16, LN)],
        [cells, maps, from_low, from_high],
        [pltpu.VMEM((ROWS, 2 * LN), jnp.float32)],
    )
    from_high = shift(to_low, "gz", -1)
    from_low = shift(to_high, "gz", 1)
    from_high_far = shift(to_low_far, "gz", -2)
    from_low_far = shift(to_high_far, "gz", 2)

    fine, coarse, to_low, to_high, to_low_far, to_high_far = call(
        share_x_kernel,
        [f32(16, 80, LN), f32(8, 40, LN), f32(480, LN), f32(400, LN), f32(40, LN), f32(40, LN)],
        [fine, coarse, from_high, from_low, from_high_far, from_low_far],
        [pltpu.VMEM((ROWS, LN), jnp.float32), pltpu.VMEM((ROWS // 2, LN), jnp.float32)],
    )
    from_high = shift(to_low, "gx", -1)
    from_low = shift(to_high, "gx", 1)
    from_high_far = shift(to_low_far, "gx", -2)
    from_low_far = shift(to_high_far, "gx", 2)

    outbox, low_band = call(
        route_kernel,
        [f32(2048, LN), f32(2, 40, 16)],
        [targets, fine, coarse, from_high, from_low, from_high_far, from_low_far],
        [pltpu.VMEM((ROWS, LN), jnp.float32), pltpu.VMEM((640, LN), jnp.float32)],
        [SM] + [VM] * 6,
    )
    inbox = lax.all_to_all(outbox.reshape(64, 32, LN), ("gx", "gy"), split_axis=0, concat_axis=0, tiled=True)

    band = low_band.reshape(2, F, 8, 16)[:, :, ::4].transpose(2, 1, 0, 3).reshape(2, F * 32)
    band = lax.all_gather(band, "gz", axis=0, tiled=True)
    turn = jnp.asarray(coarse_matrix(band.shape[0]))
    bands = jnp.dot(turn, band, precision=lax.Precision.HIGHEST)
    bands = bands.reshape(-1, F, 2, 16).transpose(1, 0, 2, 3)
    return (bands, inbox.reshape(128, 2048))


def solution(mesh):
    return jax.shard_map(
        body,
        mesh=mesh,
        in_specs=(P(None, "gz", "gx", "gy"), P("gx", "gy", "gz", None)),
        out_specs=(P(None, None, "gx", "gy"), P(("gx", "gy"), "gz")),
        check_vma=False,
    )
```

```python
import jax
import jax.numpy as jnp
import ml_dtypes
import numpy as np
from jax import lax
from jax.experimental import pallas as pl
from jax.experimental.pallas import tpu as pltpu
from jax.sharding import PartitionSpec as P

PREDICT_ONE = -1.586134342059924
UPDATE_ONE = -0.052980118572961
PREDICT_TWO = 0.882911075530934
UPDATE_TWO = 0.443506852043971
LOW_SCALE = 1.0 / 1.149604398860241
HIGH_SCALE = 1.149604398860241

F = 5
NB = 16
LN = 128
ROWS = F * NB * NB
TILES = F * NB

LOW_SIDE = (4, 6, 6)
HIGH_SIDE = (3, 5, 7)


def lift_np(values):
    low = values[0::2].copy()
    high = values[1::2].copy()
    high += PREDICT_ONE * (low + np.roll(low, -1, 0))
    low += UPDATE_ONE * (np.roll(high, 1, 0) + high)
    high += PREDICT_TWO * (low + np.roll(low, -1, 0))
    low += UPDATE_TWO * (np.roll(high, 1, 0) + high)
    joined = np.empty_like(values)
    joined[0::2] = low * LOW_SCALE
    joined[1::2] = high * HIGH_SCALE
    return joined


def split(matrix):
    matrix = np.asarray(matrix, np.float32)
    upper = matrix.astype(ml_dtypes.bfloat16)
    lower = (matrix - upper.astype(np.float32)).astype(ml_dtypes.bfloat16)
    return upper, lower


def y_matrices():
    total, start = 8 * LN, 4 * LN
    level = np.eye(total)
    maps = []
    for _ in range(3):
        level = lift_np(level)
        maps.append(level)
        level = level[0::2]
    own = np.zeros((LN, 2 * LN))
    send = np.zeros((32, LN))
    place = np.zeros((32, 2 * LN))
    columns = [lambda j: j, lambda j: LN + 2 * j, lambda j: LN + 4 * j + 1]
    at_low, at_high = 0, 16
    for depth in range(3):
        count = LN >> depth
        first = start >> depth
        block = maps[depth][:, start : start + LN]
        low, high = LOW_SIDE[depth], HIGH_SIDE[depth]
        assert not block[: first - low].any() and not block[first + count + high :].any()
        for j in range(count):
            own[:, columns[depth](j)] = block[first + j]
        for j in range(low):
            send[at_low] = block[first - low + j]
            place[at_low, columns[depth](count - low + j)] = 1
            at_low += 1
        for j in range(high):
            send[at_high] = block[first + count + j]
            place[at_high, columns[depth](j)] = 1
            at_high += 1
    return send, own, place


def lift(values):
    low = {i // 2: v for i, v in values.items() if i % 2 == 0}
    high = {i // 2: v for i, v in values.items() if i % 2 != 0}

    def add(target, source, factor, offsets):
        span = range(min(source) - 1, max(source) + 2)
        result = dict(target)
        for i in span:
            terms = [source[i + o] for o in offsets if i + o in source]
            if terms:
                step = factor * (terms[0] + terms[1] if len(terms) == 2 else terms[0])
                result[i] = result[i] + step if i in result else step
        return result

    high = add(high, low, PREDICT_ONE, (0, 1))
    low = add(low, high, UPDATE_ONE, (-1, 0))
    high = add(high, low, PREDICT_TWO, (0, 1))
    low = add(low, high, UPDATE_TWO, (-1, 0))
    joined = {2 * i: v * LOW_SCALE for i, v in low.items()}
    joined.update({2 * i + 1: v * HIGH_SCALE for i, v in high.items()})
    return joined


def lows(values):
    return {i // 2: v for i, v in values.items() if i % 2 == 0}


def dot(a, b, dims):
    return lax.dot_general(a, b, (dims, ((), ())), preferred_element_type=jnp.float32)


def halves(x):
    upper = x.astype(jnp.bfloat16)
    return upper, (x - upper.astype(jnp.float32)).astype(jnp.bfloat16)


def share_y_kernel(fields, send, maps, to_low, to_high, cells, held, matrix, sems):
    copies = [pltpu.make_async_copy(send, matrix, sems.at[F]), pltpu.make_async_copy(maps, held, sems.at[F + 1])]
    for f in range(F):
        rows = pl.ds(f * 256, 256)
        copies.append(pltpu.make_async_copy(fields.at[rows], cells.at[rows], sems.at[f]))
    for copy in copies:
        copy.start()
    copies[0].wait()
    send_hi, send_lo = matrix[:32], matrix[32:]
    dims = ((1,), (1,))
    for f in range(F):
        rows = slice(f * 256, f * 256 + 256)
        copies[2 + f].wait()
        cells_hi, cells_lo = halves(cells[rows])
        shares = dot(send_hi, cells_hi, dims) + dot(send_hi, cells_lo, dims) + dot(send_lo, cells_hi, dims)
        to_low[:, rows] = shares[:16]
        to_high[:, rows] = shares[16:]
    copies[1].wait()


def slots_kernel(writers, targets, counts):
    for i in range(64):
        counts[i] = 0
    for t in range(TILES):
        writer = writers[t]
        slot = counts[writer]
        counts[writer] = slot + 1
        targets[t] = writer * 2 + slot


def fine_shares(values):
    return lift(values)


def coarse_shares(values):
    second = lift(lows(lift(values)))
    third = lift(lows(second))
    return second, third


class Lanes:
    def __init__(self):
        self.lane = lax.broadcasted_iota(jnp.int32, (8, LN), 1)
        self.second = self.lane % 2 == 0
        self.third = self.lane % 4 == 1
        self.ahead = [self.lane % 4 == (1 + i) % 4 for i in range(4)]

    @staticmethod
    def roll(x, by):
        return pltpu.roll(x, by % LN, 1) if by % LN else x

    def pack_second(self, rows):
        packed = []
        for i in range(0, len(rows), 2):
            odd = self.roll(rows[i + 1], 1) if i + 1 < len(rows) else rows[i]
            packed.append(jnp.where(self.second, rows[i], odd))
        return packed

    def pack_third(self, rows):
        packed = rows[0]
        for i in range(1, len(rows)):
            packed = jnp.where(self.ahead[i], self.roll(rows[i], i), packed)
        return packed


def send_rows(second, third, lanes):
    near_low = lanes.pack_second([second[i - 6] for i in range(6)]) + [lanes.pack_third([third[i - 4] for i in range(4)])]
    near_high = lanes.pack_second([second[8 + i] for i in range(5)]) + [lanes.pack_third([third[4 + i] for i in range(4)])]
    return near_low, near_high, lanes.pack_third([third[-6], third[-5]]), lanes.pack_third([third[8], third[9], third[10]])


def own_y_kernel(fields, maps, own):
    cells_hi, cells_lo = halves(fields[...])
    dims = ((1,), (0,))
    own_hi, own_lo = maps[:128], maps[128:256]
    own[...] = dot(cells_hi, own_hi, dims) + dot(cells_lo, own_hi, dims) + dot(cells_hi, own_lo, dims)


def share_z_kernel(
    own, maps, from_low, from_high, fine, coarse, to_low, to_high, to_low_far, to_high_far, work
):
    low_hi, low_lo = halves(from_high[...])
    high_hi, high_lo = halves(from_low[...])
    turned = ((0,), (0,))
    place_low, place_high = maps[256:272], maps[272:]
    work[...] = (
        own[...]
        + dot(low_hi, place_low, turned)
        + dot(low_lo, place_low, turned)
        + dot(high_hi, place_high, turned)
        + dot(high_lo, place_high, turned)
    )
    lanes = Lanes()
    for f in range(F):
        for half in (0, 8):
            rows = slice(half, half + 8)
            at = [f * 256 + z * 16 + half for z in range(NB)]
            done = fine_shares({z: work[at[z] : at[z] + 8, :LN] for z in range(NB)})
            for z in range(NB):
                fine[at[z] : at[z] + 8] = done[z]
            for i in range(4):
                to_low[f, i, rows] = done[i - 4]
            for i in range(3):
                to_high[f, i, rows] = done[16 + i]
            second, third = coarse_shares({z: work[at[z] : at[z] + 8, LN:] for z in range(NB)})
            for z in range(8):
                row = jnp.where(lanes.second, second[z], third[z // 2]) if z % 2 == 0 else second[z]
                coarse[f * 128 + z * 16 + half : f * 128 + z * 16 + half + 8] = row
            near_low, near_high, far_low, far_high = send_rows(second, third, lanes)
            for i in range(4):
                to_low[f, 4 + i, rows] = near_low[i]
                to_high[f, 3 + i, rows] = near_high[i]
            to_low_far[f, rows] = far_low
            to_high_far[f, rows] = far_high


def add_coarse(base, near_low, near_high, far_low, far_high, lanes):
    zero = jnp.zeros_like(base[0])
    extra = [zero] * 8
    for i in range(6):
        extra[2 + i] = extra[2 + i] + lanes.roll(near_low[i // 2], -(i % 2))
    for i in range(5):
        extra[i] = extra[i] + lanes.roll(near_high[i // 2], -(i % 2))
    near = near_low[3] + near_high[3]
    near = near + jnp.where(lanes.ahead[3], zero, far_high)
    third = [lanes.roll(near, -r) for r in range(4)]
    third[2] = third[2] + far_low
    third[3] = third[3] + lanes.roll(far_low, -1)
    rows = []
    for i in range(8):
        other = jnp.where(lanes.third, third[i // 2], zero) if i % 2 == 0 else zero
        rows.append(base[i] + jnp.where(lanes.second, extra[i], other))
    return rows


def share_x_kernel(
    fine, coarse, from_high, from_low, from_high_far, from_low_far,
    own_fine, own_coarse, to_low, to_high, to_low_far, to_high_far, work, work_coarse,
):
    lanes = Lanes()
    for f in range(F):
        at = f * 256
        work[at : at + 48] = fine[at : at + 48] + from_low[f, :3].reshape(48, LN)
        work[at + 48 : at + 192] = fine[at + 48 : at + 192]
        work[at + 192 : at + 256] = fine[at + 192 : at + 256] + from_high[f, :4].reshape(64, LN)
        for half in (0, 8):
            rows = slice(half, half + 8)
            at = [f * 128 + z * 16 + half for z in range(8)]
            added = add_coarse(
                [coarse[at[z] : at[z] + 8] for z in range(8)],
                [from_high[f, 4 + i, rows] for i in range(4)],
                [from_low[f, 3 + i, rows] for i in range(4)],
                from_high_far[f, rows],
                from_low_far[f, rows],
                lanes,
            )
            for z in range(8):
                work_coarse[at[z] : at[z] + 8] = added[z]
    for g in range(10):
        rows = slice(g * 8, g * 8 + 8)
        done = fine_shares({x: work[pl.ds(g * 128 + x, 8, stride=16), :] for x in range(NB)})
        for x in range(NB):
            own_fine[x, rows] = done[x]
        for i in range(4):
            to_low[i * 80 + g * 8 : i * 80 + g * 8 + 8] = done[i - 4]
        for i in range(3):
            to_high[i * 80 + g * 8 : i * 80 + g * 8 + 8] = done[16 + i]
    for g in range(5):
        rows = slice(g * 8, g * 8 + 8)
        second, third = coarse_shares({x: work_coarse[pl.ds(g * 128 + x, 8, stride=16), :] for x in range(NB)})
        for x in range(8):
            own_coarse[x, rows] = jnp.where(lanes.second, second[x], third[x // 2]) if x % 2 == 0 else second[x]
        near_low, near_high, far_low, far_high = send_rows(second, third, lanes)
        for i in range(4):
            to_low[320 + i * 40 + g * 8 : 320 + i * 40 + g * 8 + 8] = near_low[i]
            to_high[240 + i * 40 + g * 8 : 240 + i * 40 + g * 8 + 8] = near_high[i]
        to_low_far[rows] = far_low
        to_high_far[rows] = far_high


def route_kernel(
    targets, fine, coarse, from_high, from_low, from_high_far, from_low_far, outbox, low_band, tiles, spread
):
    shape = (8, LN)
    lanes = Lanes()
    lane = lanes.lane
    even_row = lax.broadcasted_iota(jnp.int32, shape, 0) % 2 == 0
    replaced = (lane % 4 == 0) & even_row
    merged = lanes.second & even_row
    picked = (LN, 16)
    pick = lax.broadcasted_iota(jnp.int32, picked, 0) == 8 * lax.broadcasted_iota(jnp.int32, picked, 1) + 1
    pick = jnp.where(pick, jnp.ones(picked, jnp.float32), jnp.zeros(picked, jnp.float32)).astype(jnp.bfloat16)
    outbox[...] = jnp.zeros_like(outbox)
    for g in range(5):
        rows = slice(g * 8, g * 8 + 8)
        added = add_coarse(
            [coarse[x, rows] for x in range(8)],
            [from_high[320 + i * 40 + g * 8 : 320 + i * 40 + g * 8 + 8] for i in range(4)],
            [from_low[240 + i * 40 + g * 8 : 240 + i * 40 + g * 8 + 8] for i in range(4)],
            from_high_far[rows],
            from_low_far[rows],
            lanes,
        )
        for i, x in ((0, 0), (1, 4)):
            upper, lower = halves(added[x])
            rest = (added[x] - upper.astype(jnp.float32) - lower.astype(jnp.float32)).astype(jnp.bfloat16)
            dims = ((1,), (0,))
            low_band[i, rows] = dot(upper, pick, dims) + dot(lower, pick, dims) + dot(rest, pick, dims)
        for x in range(8):
            row = added[x]
            if x % 2 == 0:
                row = jnp.where(replaced, lanes.roll(row, -1), row)
            spread[pl.ds(x * 80 + g * 16, 8, stride=2), :] = row
            spread[pl.ds(x * 80 + g * 16 + 1, 8, stride=2), :] = row
    for g in range(10):
        rows = slice(g * 8, g * 8 + 8)
        for x in range(NB):
            row = fine[x, rows]
            if x < 3:
                row = row + from_low[x * 80 + g * 8 : x * 80 + g * 8 + 8]
            if x >= 12:
                i = x - 12
                row = row + from_high[i * 80 + g * 8 : i * 80 + g * 8 + 8]
            if x % 2 == 0:
                row = jnp.where(merged, spread[x // 2 * 80 + g * 8 : x // 2 * 80 + g * 8 + 8], row)
            tiles[pl.ds(g * 128 + x, 8, stride=16), :] = row

    for t in range(TILES):
        to = pl.multiple_of(targets[t] * 16, 16)
        outbox[pl.ds(to, 16), :] = tiles[t * 16 : t * 16 + 16]


VM = pl.BlockSpec(memory_space=pltpu.VMEM)
SM = pl.BlockSpec(memory_space=pltpu.SMEM)
HB = pl.BlockSpec(memory_space=pltpu.HBM)


def f32(*shape):
    return jax.ShapeDtypeStruct(shape, jnp.float32)


def call(kernel, outs, ins, scratch=(), specs=None, out_specs=None, flops=1 << 20, grant=32 << 20):
    moved = sum(4 * int(np.prod(a.shape)) for a in list(outs) + list(ins))
    return pl.pallas_call(
        kernel,
        out_shape=list(outs),
        in_specs=specs or [VM] * len(ins),
        out_specs=out_specs or [VM] * len(outs),
        scratch_shapes=list(scratch),
        compiler_params=pltpu.CompilerParams(vmem_limit_bytes=grant),
        cost_estimate=pl.CostEstimate(flops=flops, bytes_accessed=moved, transcendentals=0),
    )(*ins)


def shift(array, axis, by):
    count = lax.axis_size(axis)
    return lax.ppermute(array, axis, [(i, (i + by) % count) for i in range(count)])


def coarse_matrix(length):
    level_four = lift_np(np.eye(length))
    level_five = lift_np(level_four[0::2])
    level_four[0::2] = level_five
    return level_four.astype(np.float32)


def body(fields, tile_writer):
    send, own, place = y_matrices()
    send = jnp.asarray(np.concatenate(split(send)))
    maps = jnp.asarray(np.concatenate([*split(own), place.astype(ml_dtypes.bfloat16)]))
    cells = fields.reshape(ROWS, LN)

    to_low, to_high, cells, maps = call(
        share_y_kernel,
        [f32(16, ROWS), f32(16, ROWS), f32(ROWS, LN), jax.ShapeDtypeStruct(maps.shape, maps.dtype)],
        [pltpu.with_memory_space_constraint(a, pltpu.HBM) for a in (cells, send, maps)],
        [pltpu.VMEM((64, LN), jnp.bfloat16), pltpu.SemaphoreType.DMA((F + 2,))],
        [HB, HB, HB],
        grant=32 << 20,
    )
    (own,) = call(own_y_kernel, [f32(ROWS, 2 * LN)], [cells, maps], flops=1 << 30)
    from_high = shift(to_low, "gy", -1)
    from_low = shift(to_high, "gy", 1)

    (targets,) = call(
        slots_kernel,
        [jax.ShapeDtypeStruct((TILES,), jnp.int32)],
        [tile_writer.reshape(TILES)],
        [pltpu.SMEM((64,), jnp.int32)],
        [SM],
        [SM],
        flops=1 << 30,
    )
    fine, coarse, to_low, to_high, to_low_far, to_high_far = call(
        share_z_kernel,
        [f32(ROWS, LN), f32(ROWS // 2, LN), f32(F, 8, 16, LN), f32(F, 7, 16, LN), f32(F, 16, LN), f32(F, 16, LN)],
        [own, maps, from_low, from_high],
        [pltpu.VMEM((ROWS, 2 * LN), jnp.float32)],
    )
    from_high = shift(to_low, "gz", -1)
    from_low = shift(to_high, "gz", 1)
    from_high_far = shift(to_low_far, "gz", -2)
    from_low_far = shift(to_high_far, "gz", 2)

    fine, coarse, to_low, to_high, to_low_far, to_high_far = call(
        share_x_kernel,
        [f32(16, 80, LN), f32(8, 40, LN), f32(480, LN), f32(400, LN), f32(40, LN), f32(40, LN)],
        [fine, coarse, from_high, from_low, from_high_far, from_low_far],
        [pltpu.VMEM((ROWS, LN), jnp.float32), pltpu.VMEM((ROWS // 2, LN), jnp.float32)],
    )
    from_high = shift(to_low, "gx", -1)
    from_low = shift(to_high, "gx", 1)
    from_high_far = shift(to_low_far, "gx", -2)
    from_low_far = shift(to_high_far, "gx", 2)

    outbox, low_band = call(
        route_kernel,
        [f32(2048, LN), f32(2, 40, 16)],
        [targets, fine, coarse, from_high, from_low, from_high_far, from_low_far],
        [pltpu.VMEM((ROWS, LN), jnp.float32), pltpu.VMEM((640, LN), jnp.float32)],
        [SM] + [VM] * 6,
    )
    inbox = lax.all_to_all(outbox.reshape(64, 32, LN), ("gx", "gy"), split_axis=0, concat_axis=0, tiled=True)

    band = low_band.reshape(2, F, 8, 16)[:, :, ::4].transpose(2, 1, 0, 3).reshape(2, F * 32)
    band = lax.all_gather(band, "gz", axis=0, tiled=True)
    turn = jnp.asarray(coarse_matrix(band.shape[0]))
    bands = jnp.dot(turn, band, precision=lax.Precision.HIGHEST)
    bands = bands.reshape(-1, F, 2, 16).transpose(1, 0, 2, 3)
    return (bands, inbox.reshape(128, 2048))


def solution(mesh):
    return jax.shard_map(
        body,
        mesh=mesh,
        in_specs=(P(None, "gz", "gx", "gy"), P("gx", "gy", "gz", None)),
        out_specs=(P(None, None, "gx", "gy"), P(("gx", "gy"), "gz")),
        check_vma=False,
    )
```

```python
import jax
import jax.numpy as jnp
import ml_dtypes
import numpy as np
from jax import lax
from jax.experimental import pallas as pl
from jax.experimental.pallas import tpu as pltpu
from jax.sharding import PartitionSpec as P

PREDICT_ONE = -1.586134342059924
UPDATE_ONE = -0.052980118572961
PREDICT_TWO = 0.882911075530934
UPDATE_TWO = 0.443506852043971
LOW_SCALE = 1.0 / 1.149604398860241
HIGH_SCALE = 1.149604398860241

F = 5
NB = 16
LN = 128
ROWS = F * NB * NB
TILES = F * NB

LOW_SIDE = (4, 6, 6)
HIGH_SIDE = (3, 5, 7)


def lift_np(values):
    low = values[0::2].copy()
    high = values[1::2].copy()
    high += PREDICT_ONE * (low + np.roll(low, -1, 0))
    low += UPDATE_ONE * (np.roll(high, 1, 0) + high)
    high += PREDICT_TWO * (low + np.roll(low, -1, 0))
    low += UPDATE_TWO * (np.roll(high, 1, 0) + high)
    joined = np.empty_like(values)
    joined[0::2] = low * LOW_SCALE
    joined[1::2] = high * HIGH_SCALE
    return joined


def split(matrix):
    matrix = np.asarray(matrix, np.float32)
    upper = matrix.astype(ml_dtypes.bfloat16)
    lower = (matrix - upper.astype(np.float32)).astype(ml_dtypes.bfloat16)
    return upper, lower


def y_matrices():
    total, start = 8 * LN, 4 * LN
    level = np.eye(total)
    maps = []
    for _ in range(3):
        level = lift_np(level)
        maps.append(level)
        level = level[0::2]
    own = np.zeros((LN, 2 * LN))
    send = np.zeros((32, LN))
    place = np.zeros((32, 2 * LN))
    columns = [lambda j: j, lambda j: LN + 2 * j, lambda j: LN + 4 * j + 1]
    at_low, at_high = 0, 16
    for depth in range(3):
        count = LN >> depth
        first = start >> depth
        block = maps[depth][:, start : start + LN]
        low, high = LOW_SIDE[depth], HIGH_SIDE[depth]
        assert not block[: first - low].any() and not block[first + count + high :].any()
        for j in range(count):
            own[:, columns[depth](j)] = block[first + j]
        for j in range(low):
            send[at_low] = block[first - low + j]
            place[at_low, columns[depth](count - low + j)] = 1
            at_low += 1
        for j in range(high):
            send[at_high] = block[first + count + j]
            place[at_high, columns[depth](j)] = 1
            at_high += 1
    return send, own, place


def lift(values):
    low = {i // 2: v for i, v in values.items() if i % 2 == 0}
    high = {i // 2: v for i, v in values.items() if i % 2 != 0}

    def add(target, source, factor, offsets):
        span = range(min(source) - 1, max(source) + 2)
        result = dict(target)
        for i in span:
            terms = [source[i + o] for o in offsets if i + o in source]
            if terms:
                step = factor * (terms[0] + terms[1] if len(terms) == 2 else terms[0])
                result[i] = result[i] + step if i in result else step
        return result

    high = add(high, low, PREDICT_ONE, (0, 1))
    low = add(low, high, UPDATE_ONE, (-1, 0))
    high = add(high, low, PREDICT_TWO, (0, 1))
    low = add(low, high, UPDATE_TWO, (-1, 0))
    joined = {2 * i: v * LOW_SCALE for i, v in low.items()}
    joined.update({2 * i + 1: v * HIGH_SCALE for i, v in high.items()})
    return joined


def lows(values):
    return {i // 2: v for i, v in values.items() if i % 2 == 0}


def dot(a, b, dims):
    return lax.dot_general(a, b, (dims, ((), ())), preferred_element_type=jnp.float32)


def halves(x):
    upper = x.astype(jnp.bfloat16)
    return upper, (x - upper.astype(jnp.float32)).astype(jnp.bfloat16)


def share_y_kernel(fields, send, maps, to_low, to_high, cells, held, matrix, sems):
    copies = [pltpu.make_async_copy(send, matrix, sems.at[F]), pltpu.make_async_copy(maps, held, sems.at[F + 1])]
    for f in range(F):
        rows = pl.ds(f * 256, 256)
        copies.append(pltpu.make_async_copy(fields.at[rows], cells.at[rows], sems.at[f]))
    for copy in copies:
        copy.start()
    copies[0].wait()
    send_hi, send_lo = matrix[:32], matrix[32:]
    dims = ((1,), (1,))
    for f in range(F):
        rows = slice(f * 256, f * 256 + 256)
        copies[2 + f].wait()
        cells_hi, cells_lo = halves(cells[rows])
        shares = dot(send_hi, cells_hi, dims) + dot(send_hi, cells_lo, dims) + dot(send_lo, cells_hi, dims)
        to_low[:, rows] = shares[:16]
        to_high[:, rows] = shares[16:]
    copies[1].wait()


def fine_shares(values):
    return lift(values)


def coarse_shares(values):
    second = lift(lows(lift(values)))
    third = lift(lows(second))
    return second, third


class Lanes:
    def __init__(self):
        self.lane = lax.broadcasted_iota(jnp.int32, (8, LN), 1)
        self.second = self.lane % 2 == 0
        self.third = self.lane % 4 == 1
        self.ahead = [self.lane % 4 == (1 + i) % 4 for i in range(4)]

    @staticmethod
    def roll(x, by):
        return pltpu.roll(x, by % LN, 1) if by % LN else x

    def pack_second(self, rows):
        packed = []
        for i in range(0, len(rows), 2):
            odd = self.roll(rows[i + 1], 1) if i + 1 < len(rows) else rows[i]
            packed.append(jnp.where(self.second, rows[i], odd))
        return packed

    def pack_third(self, rows):
        packed = rows[0]
        for i in range(1, len(rows)):
            packed = jnp.where(self.ahead[i], self.roll(rows[i], i), packed)
        return packed


def send_rows(second, third, lanes):
    near_low = lanes.pack_second([second[i - 6] for i in range(6)]) + [lanes.pack_third([third[i - 4] for i in range(4)])]
    near_high = lanes.pack_second([second[8 + i] for i in range(5)]) + [lanes.pack_third([third[4 + i] for i in range(4)])]
    return near_low, near_high, lanes.pack_third([third[-6], third[-5]]), lanes.pack_third([third[8], third[9], third[10]])


def own_y_kernel(fields, maps, own):
    cells_hi, cells_lo = halves(fields[...])
    dims = ((1,), (0,))
    own_hi, own_lo = maps[:128], maps[128:256]
    own[...] = dot(cells_hi, own_hi, dims) + dot(cells_lo, own_hi, dims) + dot(cells_hi, own_lo, dims)


def share_z_kernel(
    own, maps, from_low, from_high, fine, coarse, to_low, to_high, to_low_far, to_high_far, work
):
    low_hi, low_lo = halves(from_high[...])
    high_hi, high_lo = halves(from_low[...])
    turned = ((0,), (0,))
    place_low, place_high = maps[256:272], maps[272:]
    work[...] = (
        own[...]
        + dot(low_hi, place_low, turned)
        + dot(low_lo, place_low, turned)
        + dot(high_hi, place_high, turned)
        + dot(high_lo, place_high, turned)
    )
    lanes = Lanes()
    for f in range(F):
        for half in (0, 8):
            rows = slice(half, half + 8)
            at = [f * 256 + z * 16 + half for z in range(NB)]
            done = fine_shares({z: work[at[z] : at[z] + 8, :LN] for z in range(NB)})
            for z in range(NB):
                fine[at[z] : at[z] + 8] = done[z]
            for i in range(4):
                to_low[f, i, rows] = done[i - 4]
            for i in range(3):
                to_high[f, i, rows] = done[16 + i]
            second, third = coarse_shares({z: work[at[z] : at[z] + 8, LN:] for z in range(NB)})
            for z in range(8):
                row = jnp.where(lanes.second, second[z], third[z // 2]) if z % 2 == 0 else second[z]
                coarse[f * 128 + z * 16 + half : f * 128 + z * 16 + half + 8] = row
            near_low, near_high, far_low, far_high = send_rows(second, third, lanes)
            for i in range(4):
                to_low[f, 4 + i, rows] = near_low[i]
                to_high[f, 3 + i, rows] = near_high[i]
            to_low_far[f, rows] = far_low
            to_high_far[f, rows] = far_high


def add_coarse(base, near_low, near_high, far_low, far_high, lanes):
    zero = jnp.zeros_like(base[0])
    extra = [zero] * 8
    for i in range(6):
        extra[2 + i] = extra[2 + i] + lanes.roll(near_low[i // 2], -(i % 2))
    for i in range(5):
        extra[i] = extra[i] + lanes.roll(near_high[i // 2], -(i % 2))
    near = near_low[3] + near_high[3]
    near = near + jnp.where(lanes.ahead[3], zero, far_high)
    third = [lanes.roll(near, -r) for r in range(4)]
    third[2] = third[2] + far_low
    third[3] = third[3] + lanes.roll(far_low, -1)
    rows = []
    for i in range(8):
        other = jnp.where(lanes.third, third[i // 2], zero) if i % 2 == 0 else zero
        rows.append(base[i] + jnp.where(lanes.second, extra[i], other))
    return rows


def fine_x_kernel(fine, from_high, from_low, own_fine, to_low, to_high, work):
    for f in range(F):
        at = f * 256
        work[at : at + 48] = fine[at : at + 48] + from_low[f, :3].reshape(48, LN)
        work[at + 48 : at + 192] = fine[at + 48 : at + 192]
        work[at + 192 : at + 256] = fine[at + 192 : at + 256] + from_high[f, :4].reshape(64, LN)
    for g in range(10):
        rows = slice(g * 8, g * 8 + 8)
        done = fine_shares({x: work[pl.ds(g * 128 + x, 8, stride=16), :] for x in range(NB)})
        for x in range(NB):
            own_fine[x, rows] = done[x]
        for i in range(4):
            to_low[i * 80 + g * 8 : i * 80 + g * 8 + 8] = done[i - 4]
        for i in range(3):
            to_high[i * 80 + g * 8 : i * 80 + g * 8 + 8] = done[16 + i]


def coarse_x_kernel(
    coarse, from_high, from_low, from_high_far, from_low_far, held_low, held_high,
    own_coarse, to_low, to_high, to_low_far, to_high_far, work_coarse,
):
    del held_low, held_high
    lanes = Lanes()
    for f in range(F):
        for half in (0, 8):
            rows = slice(half, half + 8)
            at = [f * 128 + z * 16 + half for z in range(8)]
            added = add_coarse(
                [coarse[at[z] : at[z] + 8] for z in range(8)],
                [from_high[f, 4 + i, rows] for i in range(4)],
                [from_low[f, 3 + i, rows] for i in range(4)],
                from_high_far[f, rows],
                from_low_far[f, rows],
                lanes,
            )
            for z in range(8):
                work_coarse[at[z] : at[z] + 8] = added[z]
    for g in range(5):
        rows = slice(g * 8, g * 8 + 8)
        second, third = coarse_shares({x: work_coarse[pl.ds(g * 128 + x, 8, stride=16), :] for x in range(NB)})
        for x in range(8):
            own_coarse[x, rows] = jnp.where(lanes.second, second[x], third[x // 2]) if x % 2 == 0 else second[x]
        near_low, near_high, far_low, far_high = send_rows(second, third, lanes)
        for i in range(4):
            to_low[320 + i * 40 + g * 8 : 320 + i * 40 + g * 8 + 8] = near_low[i]
            to_high[240 + i * 40 + g * 8 : 240 + i * 40 + g * 8 + 8] = near_high[i]
        to_low_far[rows] = far_low
        to_high_far[rows] = far_high


def tiles_kernel(writers, fine, from_high, from_low, targets, tiles, counts):
    for i in range(64):
        counts[i] = 0
    for t in range(TILES):
        writer = writers[t]
        slot = counts[writer]
        counts[writer] = slot + 1
        targets[t] = writer * 2 + slot
    for g in range(10):
        rows = slice(g * 8, g * 8 + 8)
        for x in range(NB):
            row = fine[x, rows]
            if x < 3:
                row = row + from_low[x * 80 + g * 8 : x * 80 + g * 8 + 8]
            if x >= 12:
                i = x - 12
                row = row + from_high[i * 80 + g * 8 : i * 80 + g * 8 + 8]
            tiles[pl.ds(g * 128 + x, 8, stride=16), :] = row


def route_kernel(
    targets, tiles, coarse, from_high, from_low, from_high_far, from_low_far, outbox, low_band, spread
):
    shape = (8, LN)
    lanes = Lanes()
    even_row = lax.broadcasted_iota(jnp.int32, shape, 0) % 2 == 0
    replaced = (lanes.lane % 4 == 0) & even_row
    merged = lanes.second & even_row
    picked = (LN, 16)
    pick = lax.broadcasted_iota(jnp.int32, picked, 0) == 8 * lax.broadcasted_iota(jnp.int32, picked, 1) + 1
    pick = jnp.where(pick, jnp.ones(picked, jnp.float32), jnp.zeros(picked, jnp.float32)).astype(jnp.bfloat16)
    outbox[...] = jnp.zeros_like(outbox)
    for g in range(5):
        rows = slice(g * 8, g * 8 + 8)
        added = add_coarse(
            [coarse[x, rows] for x in range(8)],
            [from_high[320 + i * 40 + g * 8 : 320 + i * 40 + g * 8 + 8] for i in range(4)],
            [from_low[240 + i * 40 + g * 8 : 240 + i * 40 + g * 8 + 8] for i in range(4)],
            from_high_far[rows],
            from_low_far[rows],
            lanes,
        )
        for i, x in ((0, 0), (1, 4)):
            upper, lower = halves(added[x])
            rest = (added[x] - upper.astype(jnp.float32) - lower.astype(jnp.float32)).astype(jnp.bfloat16)
            dims = ((1,), (0,))
            low_band[i, rows] = dot(upper, pick, dims) + dot(lower, pick, dims) + dot(rest, pick, dims)
        for x in range(8):
            row = added[x]
            if x % 2 == 0:
                row = jnp.where(replaced, lanes.roll(row, -1), row)
            for odd in range(2):
                spread[pl.ds(g * 128 + 2 * x + odd, 8, stride=16), :] = row
    for t in range(TILES):
        to = pl.multiple_of(targets[t] * 16, 16)
        f, z = t // NB, t % NB
        for half in (0, 8):
            row = tiles[t * 16 + half : t * 16 + half + 8]
            if z % 2 == 0:
                at = (f * 8 + z // 2) * 16 + half
                row = jnp.where(merged, spread[at : at + 8], row)
            outbox[pl.ds(to + half, 8), :] = row


VM = pl.BlockSpec(memory_space=pltpu.VMEM)
SM = pl.BlockSpec(memory_space=pltpu.SMEM)
HB = pl.BlockSpec(memory_space=pltpu.HBM)


def f32(*shape):
    return jax.ShapeDtypeStruct(shape, jnp.float32)


def call(kernel, outs, ins, scratch=(), specs=None, out_specs=None, flops=1 << 20, grant=32 << 20, aliases=None):
    moved = sum(4 * int(np.prod(a.shape)) for a in list(outs) + list(ins))
    return pl.pallas_call(
        kernel,
        out_shape=list(outs),
        in_specs=specs or [VM] * len(ins),
        out_specs=out_specs or [VM] * len(outs),
        scratch_shapes=list(scratch),
        input_output_aliases=aliases or {},
        compiler_params=pltpu.CompilerParams(vmem_limit_bytes=grant),
        cost_estimate=pl.CostEstimate(flops=flops, bytes_accessed=moved, transcendentals=0),
    )(*ins)


def shift(array, axis, by):
    count = lax.axis_size(axis)
    return lax.ppermute(array, axis, [(i, (i + by) % count) for i in range(count)])


def coarse_matrix(length):
    level_four = lift_np(np.eye(length))
    level_five = lift_np(level_four[0::2])
    level_four[0::2] = level_five
    return level_four.astype(np.float32)


def body(fields, tile_writer):
    send, own, place = y_matrices()
    send = jnp.asarray(np.concatenate(split(send)))
    maps = jnp.asarray(np.concatenate([*split(own), place.astype(ml_dtypes.bfloat16)]))
    cells = fields.reshape(ROWS, LN)

    to_low, to_high, cells, maps = call(
        share_y_kernel,
        [f32(16, ROWS), f32(16, ROWS), f32(ROWS, LN), jax.ShapeDtypeStruct(maps.shape, maps.dtype)],
        [pltpu.with_memory_space_constraint(a, pltpu.HBM) for a in (cells, send, maps)],
        [pltpu.VMEM((64, LN), jnp.bfloat16), pltpu.SemaphoreType.DMA((F + 2,))],
        [HB, HB, HB],
        grant=32 << 20,
    )
    (own,) = call(own_y_kernel, [f32(ROWS, 2 * LN)], [cells, maps], flops=1 << 30)
    from_high = shift(to_low, "gy", -1)
    from_low = shift(to_high, "gy", 1)

    fine, coarse, to_low, to_high, to_low_far, to_high_far = call(
        share_z_kernel,
        [f32(ROWS, LN), f32(ROWS // 2, LN), f32(F, 8, 16, LN), f32(F, 7, 16, LN), f32(F, 16, LN), f32(F, 16, LN)],
        [own, maps, from_low, from_high],
        [pltpu.VMEM((ROWS, 2 * LN), jnp.float32)],
    )
    from_high = shift(to_low, "gz", -1)
    from_low = shift(to_high, "gz", 1)
    from_high_far = shift(to_low_far, "gz", -2)
    from_low_far = shift(to_high_far, "gz", 2)

    fine, to_low, to_high = call(
        fine_x_kernel,
        [f32(16, 80, LN), f32(480, LN), f32(400, LN)],
        [fine, from_high, from_low],
        [pltpu.VMEM((ROWS, LN), jnp.float32)],
        flops=1 << 30,
    )
    coarse, to_low, to_high, to_low_far, to_high_far = call(
        coarse_x_kernel,
        [f32(8, 40, LN), f32(480, LN), f32(400, LN), f32(40, LN), f32(40, LN)],
        [coarse, from_high, from_low, from_high_far, from_low_far, to_low, to_high],
        [pltpu.VMEM((ROWS // 2, LN), jnp.float32)],
        aliases={5: 1, 6: 2},
    )
    from_high = shift(to_low, "gx", -1)
    from_low = shift(to_high, "gx", 1)
    from_high_far = shift(to_low_far, "gx", -2)
    from_low_far = shift(to_high_far, "gx", 2)

    targets, tiles = call(
        tiles_kernel,
        [jax.ShapeDtypeStruct((TILES,), jnp.int32), f32(ROWS, LN)],
        [tile_writer.reshape(TILES), fine, from_high, from_low],
        [pltpu.SMEM((64,), jnp.int32)],
        [SM, VM, VM, VM],
        [SM, VM],
        flops=1 << 30,
    )
    outbox, low_band = call(
        route_kernel,
        [f32(2048, LN), f32(2, 40, 16)],
        [targets, tiles, coarse, from_high, from_low, from_high_far, from_low_far],
        [pltpu.VMEM((640, LN), jnp.float32)],
        [SM] + [VM] * 6,
    )
    inbox = lax.all_to_all(outbox.reshape(64, 32, LN), ("gx", "gy"), split_axis=0, concat_axis=0, tiled=True)

    band = low_band.reshape(2, F, 8, 16)[:, :, ::4].transpose(2, 1, 0, 3).reshape(2, F * 32)
    band = lax.all_gather(band, "gz", axis=0, tiled=True)
    turn = jnp.asarray(coarse_matrix(band.shape[0]))
    bands = jnp.dot(turn, band, precision=lax.Precision.HIGHEST)
    bands = bands.reshape(-1, F, 2, 16).transpose(1, 0, 2, 3)
    return (bands, inbox.reshape(128, 2048))


def solution(mesh):
    return jax.shard_map(
        body,
        mesh=mesh,
        in_specs=(P(None, "gz", "gx", "gy"), P("gx", "gy", "gz", None)),
        out_specs=(P(None, None, "gx", "gy"), P(("gx", "gy"), "gz")),
        check_vma=False,
    )
```

```python
import jax
import jax.numpy as jnp
import ml_dtypes
import numpy as np
from jax import lax
from jax.experimental import pallas as pl
from jax.experimental.pallas import tpu as pltpu
from jax.sharding import PartitionSpec as P

PREDICT_ONE = -1.586134342059924
UPDATE_ONE = -0.052980118572961
PREDICT_TWO = 0.882911075530934
UPDATE_TWO = 0.443506852043971
LOW_SCALE = 1.0 / 1.149604398860241
HIGH_SCALE = 1.149604398860241

F = 5
NB = 16
LN = 128
ROWS = F * NB * NB
TILES = F * NB

LOW_SIDE = (4, 6, 6)
HIGH_SIDE = (3, 5, 7)


def lift_np(values):
    low = values[0::2].copy()
    high = values[1::2].copy()
    high += PREDICT_ONE * (low + np.roll(low, -1, 0))
    low += UPDATE_ONE * (np.roll(high, 1, 0) + high)
    high += PREDICT_TWO * (low + np.roll(low, -1, 0))
    low += UPDATE_TWO * (np.roll(high, 1, 0) + high)
    joined = np.empty_like(values)
    joined[0::2] = low * LOW_SCALE
    joined[1::2] = high * HIGH_SCALE
    return joined


def split(matrix):
    matrix = np.asarray(matrix, np.float32)
    upper = matrix.astype(ml_dtypes.bfloat16)
    lower = (matrix - upper.astype(np.float32)).astype(ml_dtypes.bfloat16)
    return upper, lower


def y_matrices():
    total, start = 8 * LN, 4 * LN
    level = np.eye(total)
    maps = []
    for _ in range(3):
        level = lift_np(level)
        maps.append(level)
        level = level[0::2]
    own = np.zeros((LN, 2 * LN))
    send = np.zeros((32, LN))
    place = np.zeros((32, 2 * LN))
    columns = [lambda j: j, lambda j: LN + 2 * j, lambda j: LN + 4 * j + 1]
    at_low, at_high = 0, 16
    for depth in range(3):
        count = LN >> depth
        first = start >> depth
        block = maps[depth][:, start : start + LN]
        low, high = LOW_SIDE[depth], HIGH_SIDE[depth]
        assert not block[: first - low].any() and not block[first + count + high :].any()
        for j in range(count):
            own[:, columns[depth](j)] = block[first + j]
        for j in range(low):
            send[at_low] = block[first - low + j]
            place[at_low, columns[depth](count - low + j)] = 1
            at_low += 1
        for j in range(high):
            send[at_high] = block[first + count + j]
            place[at_high, columns[depth](j)] = 1
            at_high += 1
    return send, own, place


def lift(values):
    low = {i // 2: v for i, v in values.items() if i % 2 == 0}
    high = {i // 2: v for i, v in values.items() if i % 2 != 0}

    def add(target, source, factor, offsets):
        span = range(min(source) - 1, max(source) + 2)
        result = dict(target)
        for i in span:
            terms = [source[i + o] for o in offsets if i + o in source]
            if terms:
                step = factor * (terms[0] + terms[1] if len(terms) == 2 else terms[0])
                result[i] = result[i] + step if i in result else step
        return result

    high = add(high, low, PREDICT_ONE, (0, 1))
    low = add(low, high, UPDATE_ONE, (-1, 0))
    high = add(high, low, PREDICT_TWO, (0, 1))
    low = add(low, high, UPDATE_TWO, (-1, 0))
    joined = {2 * i: v * LOW_SCALE for i, v in low.items()}
    joined.update({2 * i + 1: v * HIGH_SCALE for i, v in high.items()})
    return joined


def lows(values):
    return {i // 2: v for i, v in values.items() if i % 2 == 0}


def dot(a, b, dims):
    return lax.dot_general(a, b, (dims, ((), ())), preferred_element_type=jnp.float32)


def halves(x):
    upper = x.astype(jnp.bfloat16)
    return upper, (x - upper.astype(jnp.float32)).astype(jnp.bfloat16)


def share_y_kernel(fields, send, maps, to_low, to_high, cells, held, matrix, sems):
    copies = [pltpu.make_async_copy(send, matrix, sems.at[F])]
    for f in range(F):
        rows = pl.ds(f * 256, 256)
        copies.append(pltpu.make_async_copy(fields.at[rows], cells.at[rows], sems.at[f]))
    copies.append(pltpu.make_async_copy(maps, held, sems.at[F + 1]))
    for copy in copies:
        copy.start()
    copies[0].wait()
    both, send_hi = matrix[...], matrix[:32]
    dims = ((1,), (1,))
    for f in range(F):
        rows = slice(f * 256, f * 256 + 256)
        copies[1 + f].wait()
        cells_hi, cells_lo = halves(cells[rows])
        upper = dot(both, cells_hi, dims)
        shares = upper[:32] + dot(send_hi, cells_lo, dims) + upper[32:]
        to_low[:, rows] = shares[:16]
        to_high[:, rows] = shares[16:]
    copies[F + 1].wait()


def fine_shares(values):
    return lift(values)


def coarse_shares(values):
    second = lift(lows(lift(values)))
    third = lift(lows(second))
    return second, third


class Lanes:
    def __init__(self):
        self.lane = lax.broadcasted_iota(jnp.int32, (8, LN), 1)
        self.second = self.lane % 2 == 0
        self.third = self.lane % 4 == 1
        self.ahead = [self.lane % 4 == (1 + i) % 4 for i in range(4)]

    @staticmethod
    def roll(x, by):
        return pltpu.roll(x, by % LN, 1) if by % LN else x

    def pack_second(self, rows):
        packed = []
        for i in range(0, len(rows), 2):
            odd = self.roll(rows[i + 1], 1) if i + 1 < len(rows) else rows[i]
            packed.append(jnp.where(self.second, rows[i], odd))
        return packed

    def pack_third(self, rows):
        packed = rows[0]
        for i in range(1, len(rows)):
            packed = jnp.where(self.ahead[i], self.roll(rows[i], i), packed)
        return packed


def send_rows(second, third, lanes):
    near_low = lanes.pack_second([second[i - 6] for i in range(6)]) + [lanes.pack_third([third[i - 4] for i in range(4)])]
    near_high = lanes.pack_second([second[8 + i] for i in range(5)]) + [lanes.pack_third([third[4 + i] for i in range(4)])]
    return near_low, near_high, lanes.pack_third([third[-6], third[-5]]), lanes.pack_third([third[8], third[9], third[10]])


def own_y_kernel(fields, maps, own, outbox, zeros, sems):
    zeros[...] = jnp.zeros_like(zeros)
    copies = [pltpu.make_async_copy(zeros, outbox.at[pl.ds(i * 512, 512)], sems.at[i]) for i in range(4)]
    for copy in copies:
        copy.start()
    cells_hi, cells_lo = halves(fields[...])
    dims = ((1,), (0,))
    own_hi, own_lo = maps[:128], maps[128:256]
    own[...] = dot(cells_hi, own_hi, dims) + dot(cells_lo, own_hi, dims) + dot(cells_hi, own_lo, dims)
    for copy in copies:
        copy.wait()


def share_z_kernel(
    own, maps, from_low, from_high, fine, coarse, to_low, to_high, to_low_far, to_high_far, work
):
    low_hi, low_lo = halves(from_high[...])
    high_hi, high_lo = halves(from_low[...])
    turned = ((0,), (0,))
    place_low, place_high = maps[256:272], maps[272:]
    work[...] = (
        own[...]
        + dot(low_hi, place_low, turned)
        + dot(low_lo, place_low, turned)
        + dot(high_hi, place_high, turned)
        + dot(high_lo, place_high, turned)
    )
    lanes = Lanes()
    for f in range(F):
        for half in (0, 8):
            rows = slice(half, half + 8)
            at = [f * 256 + z * 16 + half for z in range(NB)]
            done = fine_shares({z: work[at[z] : at[z] + 8, :LN] for z in range(NB)})
            for z in range(NB):
                fine[at[z] : at[z] + 8] = done[z]
            for i in range(4):
                to_low[f, i, rows] = done[i - 4]
            for i in range(3):
                to_high[f, i, rows] = done[16 + i]
            second, third = coarse_shares({z: work[at[z] : at[z] + 8, LN:] for z in range(NB)})
            for z in range(8):
                row = jnp.where(lanes.second, second[z], third[z // 2]) if z % 2 == 0 else second[z]
                coarse[f * 128 + z * 16 + half : f * 128 + z * 16 + half + 8] = row
            near_low, near_high, far_low, far_high = send_rows(second, third, lanes)
            for i in range(4):
                to_low[f, 4 + i, rows] = near_low[i]
                to_high[f, 3 + i, rows] = near_high[i]
            to_low_far[f, rows] = far_low
            to_high_far[f, rows] = far_high


def add_coarse(base, near_low, near_high, far_low, far_high, lanes):
    zero = jnp.zeros_like(base[0])
    extra = [zero] * 8
    for i in range(6):
        extra[2 + i] = extra[2 + i] + lanes.roll(near_low[i // 2], -(i % 2))
    for i in range(5):
        extra[i] = extra[i] + lanes.roll(near_high[i // 2], -(i % 2))
    near = near_low[3] + near_high[3]
    near = near + jnp.where(lanes.ahead[3], zero, far_high)
    third = [lanes.roll(near, -r) for r in range(4)]
    third[2] = third[2] + far_low
    third[3] = third[3] + lanes.roll(far_low, -1)
    rows = []
    for i in range(8):
        other = jnp.where(lanes.third, third[i // 2], zero) if i % 2 == 0 else zero
        rows.append(base[i] + jnp.where(lanes.second, extra[i], other))
    return rows


def fine_x_kernel(fine, from_high, from_low, own_fine, to_low, to_high, work):
    for f in range(F):
        at = f * 256
        work[at : at + 48] = fine[at : at + 48] + from_low[f, :3].reshape(48, LN)
        work[at + 48 : at + 192] = fine[at + 48 : at + 192]
        work[at + 192 : at + 256] = fine[at + 192 : at + 256] + from_high[f, :4].reshape(64, LN)
    for g in range(10):
        rows = slice(g * 8, g * 8 + 8)
        done = fine_shares({x: work[pl.ds(g * 128 + x, 8, stride=16), :] for x in range(NB)})
        for x in range(NB):
            own_fine[x, rows] = done[x]
        for i in range(4):
            to_low[i * 80 + g * 8 : i * 80 + g * 8 + 8] = done[i - 4]
        for i in range(3):
            to_high[i * 80 + g * 8 : i * 80 + g * 8 + 8] = done[16 + i]


def coarse_x_kernel(
    coarse, from_high, from_low, from_high_far, from_low_far, held_low, held_high,
    own_coarse, to_low, to_high, to_low_far, to_high_far, work_coarse,
):
    del held_low, held_high
    lanes = Lanes()
    for f in range(F):
        for half in (0, 8):
            rows = slice(half, half + 8)
            at = [f * 128 + z * 16 + half for z in range(8)]
            added = add_coarse(
                [coarse[at[z] : at[z] + 8] for z in range(8)],
                [from_high[f, 4 + i, rows] for i in range(4)],
                [from_low[f, 3 + i, rows] for i in range(4)],
                from_high_far[f, rows],
                from_low_far[f, rows],
                lanes,
            )
            for z in range(8):
                work_coarse[at[z] : at[z] + 8] = added[z]
    for g in range(5):
        rows = slice(g * 8, g * 8 + 8)
        second, third = coarse_shares({x: work_coarse[pl.ds(g * 128 + x, 8, stride=16), :] for x in range(NB)})
        for x in range(8):
            own_coarse[x, rows] = jnp.where(lanes.second, second[x], third[x // 2]) if x % 2 == 0 else second[x]
        near_low, near_high, far_low, far_high = send_rows(second, third, lanes)
        for i in range(4):
            to_low[320 + i * 40 + g * 8 : 320 + i * 40 + g * 8 + 8] = near_low[i]
            to_high[240 + i * 40 + g * 8 : 240 + i * 40 + g * 8 + 8] = near_high[i]
        to_low_far[rows] = far_low
        to_high_far[rows] = far_high


def tile_copies(targets, tiles, outbox, sems, first):
    copies = []
    for i in range(TILES // 2):
        t = 2 * i + first
        to = pl.multiple_of(targets[t] * 16, 16)
        copies.append(pltpu.make_async_copy(tiles.at[pl.ds(t * 16, 16)], outbox.at[pl.ds(to, 16)], sems.at[i]))
    return copies


def tiles_kernel(writers, fine, from_high, from_low, cleared, targets, tiles, outbox, counts, sems):
    del cleared
    for i in range(64):
        counts[i] = 0
    for t in range(TILES):
        writer = writers[t]
        slot = counts[writer]
        counts[writer] = slot + 1
        targets[t] = writer * 2 + slot
    for g in range(10):
        rows = slice(g * 8, g * 8 + 8)
        for x in range(NB):
            row = fine[x, rows]
            if x < 3:
                row = row + from_low[x * 80 + g * 8 : x * 80 + g * 8 + 8]
            if x >= 12:
                i = x - 12
                row = row + from_high[i * 80 + g * 8 : i * 80 + g * 8 + 8]
            tiles[pl.ds(g * 128 + x, 8, stride=16), :] = row
    copies = tile_copies(targets, tiles, outbox, sems, 1)
    for copy in copies:
        copy.start()
    for copy in copies:
        copy.wait()


def route_kernel(
    targets, tiles, coarse, from_high, from_low, from_high_far, from_low_far, filled,
    outbox, low_band, spread, whole, sems,
):
    del filled
    copies = tile_copies(targets, whole, outbox, sems, 0)
    shape = (8, LN)
    lanes = Lanes()
    even_row = lax.broadcasted_iota(jnp.int32, shape, 0) % 2 == 0
    replaced = (lanes.lane % 4 == 0) & even_row
    merged = lanes.second & even_row
    picked = (LN, 16)
    pick = lax.broadcasted_iota(jnp.int32, picked, 0) == 8 * lax.broadcasted_iota(jnp.int32, picked, 1) + 1
    pick = jnp.where(pick, jnp.ones(picked, jnp.float32), jnp.zeros(picked, jnp.float32)).astype(jnp.bfloat16)
    for g in range(5):
        rows = slice(g * 8, g * 8 + 8)
        added = add_coarse(
            [coarse[x, rows] for x in range(8)],
            [from_high[320 + i * 40 + g * 8 : 320 + i * 40 + g * 8 + 8] for i in range(4)],
            [from_low[240 + i * 40 + g * 8 : 240 + i * 40 + g * 8 + 8] for i in range(4)],
            from_high_far[rows],
            from_low_far[rows],
            lanes,
        )
        for x in range(8):
            row = added[x]
            if x % 2 == 0:
                row = jnp.where(replaced, lanes.roll(row, -1), row)
            for odd in range(2):
                spread[pl.ds(g * 128 + 2 * x + odd, 8, stride=16), :] = row
        for z in range(0, NB, 2):
            t = g * NB + z
            for half in (0, 8):
                at = (g * 8 + z // 2) * 16 + half
                here = slice(t * 16 + half, t * 16 + half + 8)
                whole[here] = jnp.where(merged, spread[at : at + 8], tiles[here])
            copies[t // 2].start()
        for i, x in ((0, 0), (1, 4)):
            upper, lower = halves(added[x])
            rest = (added[x] - upper.astype(jnp.float32) - lower.astype(jnp.float32)).astype(jnp.bfloat16)
            dims = ((1,), (0,))
            low_band[i, rows] = dot(upper, pick, dims) + dot(lower, pick, dims) + dot(rest, pick, dims)
    for copy in copies:
        copy.wait()


VM = pl.BlockSpec(memory_space=pltpu.VMEM)
SM = pl.BlockSpec(memory_space=pltpu.SMEM)
HB = pl.BlockSpec(memory_space=pltpu.HBM)


def f32(*shape):
    return jax.ShapeDtypeStruct(shape, jnp.float32)


def call(kernel, outs, ins, scratch=(), specs=None, out_specs=None, flops=1 << 20, grant=32 << 20, aliases=None):
    moved = sum(4 * int(np.prod(a.shape)) for a in list(outs) + list(ins))
    return pl.pallas_call(
        kernel,
        out_shape=list(outs),
        in_specs=specs or [VM] * len(ins),
        out_specs=out_specs or [VM] * len(outs),
        scratch_shapes=list(scratch),
        input_output_aliases=aliases or {},
        compiler_params=pltpu.CompilerParams(vmem_limit_bytes=grant),
        cost_estimate=pl.CostEstimate(flops=flops, bytes_accessed=moved, transcendentals=0),
    )(*ins)


def shift(array, axis, by):
    count = lax.axis_size(axis)
    return lax.ppermute(array, axis, [(i, (i + by) % count) for i in range(count)])


def coarse_matrix(length):
    level_four = lift_np(np.eye(length))
    level_five = lift_np(level_four[0::2])
    level_four[0::2] = level_five
    return level_four.astype(np.float32)


def body(fields, tile_writer):
    send, own, place = y_matrices()
    send = jnp.asarray(np.concatenate(split(send)))
    maps = jnp.asarray(np.concatenate([*split(own), place.astype(ml_dtypes.bfloat16)]))
    cells = fields.reshape(ROWS, LN)

    to_low, to_high, cells, maps = call(
        share_y_kernel,
        [f32(16, ROWS), f32(16, ROWS), f32(ROWS, LN), jax.ShapeDtypeStruct(maps.shape, maps.dtype)],
        [pltpu.with_memory_space_constraint(a, pltpu.HBM) for a in (cells, send, maps)],
        [pltpu.VMEM((64, LN), jnp.bfloat16), pltpu.SemaphoreType.DMA((F + 2,))],
        [HB, HB, HB],
        grant=32 << 20,
    )
    own, outbox = call(
        own_y_kernel,
        [f32(ROWS, 2 * LN), f32(2048, LN)],
        [cells, maps],
        [pltpu.VMEM((512, LN), jnp.float32), pltpu.SemaphoreType.DMA((4,))],
        out_specs=[VM, HB],
        flops=1 << 30,
    )
    from_high = shift(to_low, "gy", -1)
    from_low = shift(to_high, "gy", 1)

    fine, coarse, to_low, to_high, to_low_far, to_high_far = call(
        share_z_kernel,
        [f32(ROWS, LN), f32(ROWS // 2, LN), f32(F, 8, 16, LN), f32(F, 7, 16, LN), f32(F, 16, LN), f32(F, 16, LN)],
        [own, maps, from_low, from_high],
        [pltpu.VMEM((ROWS, 2 * LN), jnp.float32)],
    )
    from_high = shift(to_low, "gz", -1)
    from_low = shift(to_high, "gz", 1)
    from_high_far = shift(to_low_far, "gz", -2)
    from_low_far = shift(to_high_far, "gz", 2)

    fine, to_low, to_high = call(
        fine_x_kernel,
        [f32(16, 80, LN), f32(480, LN), f32(400, LN)],
        [fine, from_high, from_low],
        [pltpu.VMEM((ROWS, LN), jnp.float32)],
        flops=1 << 30,
    )
    coarse, to_low, to_high, to_low_far, to_high_far = call(
        coarse_x_kernel,
        [f32(8, 40, LN), f32(480, LN), f32(400, LN), f32(40, LN), f32(40, LN)],
        [coarse, from_high, from_low, from_high_far, from_low_far, to_low, to_high],
        [pltpu.VMEM((ROWS // 2, LN), jnp.float32)],
        aliases={5: 1, 6: 2},
    )
    from_high = shift(to_low, "gx", -1)
    from_low = shift(to_high, "gx", 1)
    from_high_far = shift(to_low_far, "gx", -2)
    from_low_far = shift(to_high_far, "gx", 2)

    targets, tiles, outbox = call(
        tiles_kernel,
        [jax.ShapeDtypeStruct((TILES,), jnp.int32), f32(ROWS, LN), f32(2048, LN)],
        [tile_writer.reshape(TILES), fine, from_high, from_low, outbox],
        [pltpu.SMEM((64,), jnp.int32), pltpu.SemaphoreType.DMA((TILES // 2,))],
        [SM, VM, VM, VM, HB],
        [SM, VM, HB],
        flops=1 << 30,
        aliases={4: 2},
    )
    outbox, low_band = call(
        route_kernel,
        [f32(2048, LN), f32(2, 40, 16)],
        [targets, tiles, coarse, from_high, from_low, from_high_far, from_low_far, outbox],
        [pltpu.VMEM((640, LN), jnp.float32), pltpu.VMEM((ROWS, LN), jnp.float32), pltpu.SemaphoreType.DMA((TILES // 2,))],
        [SM] + [VM] * 6 + [HB],
        [HB, VM],
        aliases={7: 0},
    )
    inbox = lax.all_to_all(outbox.reshape(64, 32, LN), ("gx", "gy"), split_axis=0, concat_axis=0, tiled=True)

    band = low_band.reshape(2, F, 8, 16)[:, :, ::4].transpose(2, 1, 0, 3).reshape(2, F * 32)
    band = lax.all_gather(band, "gz", axis=0, tiled=True)
    turn = jnp.asarray(coarse_matrix(band.shape[0]))
    bands = jnp.dot(turn, band, precision=lax.Precision.HIGHEST)
    bands = bands.reshape(-1, F, 2, 16).transpose(1, 0, 2, 3)
    return (bands, inbox.reshape(128, 2048))


def solution(mesh):
    return jax.shard_map(
        body,
        mesh=mesh,
        in_specs=(P(None, "gz", "gx", "gy"), P("gx", "gy", "gz", None)),
        out_specs=(P(None, None, "gx", "gy"), P(("gx", "gy"), "gz")),
        check_vma=False,
    )
```

```python
import jax
import jax.numpy as jnp
import ml_dtypes
import numpy as np
from jax import lax
from jax.experimental import pallas as pl
from jax.experimental.pallas import tpu as pltpu
from jax.sharding import PartitionSpec as P

PREDICT_ONE = -1.586134342059924
UPDATE_ONE = -0.052980118572961
PREDICT_TWO = 0.882911075530934
UPDATE_TWO = 0.443506852043971
LOW_SCALE = 1.0 / 1.149604398860241
HIGH_SCALE = 1.149604398860241

F = 5
NB = 16
LN = 128
ROWS = F * NB * NB
TILES = F * NB

LOW_SIDE = (4, 6, 6)
HIGH_SIDE = (3, 5, 7)


def lift_np(values):
    low = values[0::2].copy()
    high = values[1::2].copy()
    high += PREDICT_ONE * (low + np.roll(low, -1, 0))
    low += UPDATE_ONE * (np.roll(high, 1, 0) + high)
    high += PREDICT_TWO * (low + np.roll(low, -1, 0))
    low += UPDATE_TWO * (np.roll(high, 1, 0) + high)
    joined = np.empty_like(values)
    joined[0::2] = low * LOW_SCALE
    joined[1::2] = high * HIGH_SCALE
    return joined


def split(matrix):
    matrix = np.asarray(matrix, np.float32)
    upper = matrix.astype(ml_dtypes.bfloat16)
    lower = (matrix - upper.astype(np.float32)).astype(ml_dtypes.bfloat16)
    return upper, lower


def y_matrices():
    total, start = 8 * LN, 4 * LN
    level = np.eye(total)
    maps = []
    for _ in range(3):
        level = lift_np(level)
        maps.append(level)
        level = level[0::2]
    own = np.zeros((LN, 2 * LN))
    send = np.zeros((32, LN))
    place = np.zeros((32, 2 * LN))
    columns = [lambda j: j, lambda j: LN + 2 * j, lambda j: LN + 4 * j + 1]
    at_low, at_high = 0, 16
    for depth in range(3):
        count = LN >> depth
        first = start >> depth
        block = maps[depth][:, start : start + LN]
        low, high = LOW_SIDE[depth], HIGH_SIDE[depth]
        assert not block[: first - low].any() and not block[first + count + high :].any()
        for j in range(count):
            own[:, columns[depth](j)] = block[first + j]
        for j in range(low):
            send[at_low] = block[first - low + j]
            place[at_low, columns[depth](count - low + j)] = 1
            at_low += 1
        for j in range(high):
            send[at_high] = block[first + count + j]
            place[at_high, columns[depth](j)] = 1
            at_high += 1
    return send, own, place


def lift(values):
    low = {i // 2: v for i, v in values.items() if i % 2 == 0}
    high = {i // 2: v for i, v in values.items() if i % 2 != 0}

    def add(target, source, factor, offsets):
        span = range(min(source) - 1, max(source) + 2)
        result = dict(target)
        for i in span:
            terms = [source[i + o] for o in offsets if i + o in source]
            if terms:
                step = factor * (terms[0] + terms[1] if len(terms) == 2 else terms[0])
                result[i] = result[i] + step if i in result else step
        return result

    high = add(high, low, PREDICT_ONE, (0, 1))
    low = add(low, high, UPDATE_ONE, (-1, 0))
    high = add(high, low, PREDICT_TWO, (0, 1))
    low = add(low, high, UPDATE_TWO, (-1, 0))
    joined = {2 * i: v * LOW_SCALE for i, v in low.items()}
    joined.update({2 * i + 1: v * HIGH_SCALE for i, v in high.items()})
    return joined


def lows(values):
    return {i // 2: v for i, v in values.items() if i % 2 == 0}


def dot(a, b, dims):
    return lax.dot_general(a, b, (dims, ((), ())), preferred_element_type=jnp.float32)


def halves(x):
    upper = x.astype(jnp.bfloat16)
    return upper, (x - upper.astype(jnp.float32)).astype(jnp.bfloat16)


def share_y_kernel(fields, send, maps, writers, to_low, to_high, cells, held, held_writers, matrix, sems):
    copies = [pltpu.make_async_copy(send, matrix, sems.at[F])]
    for f in range(F):
        rows = pl.ds(f * 256, 256)
        copies.append(pltpu.make_async_copy(fields.at[rows], cells.at[rows], sems.at[f]))
    copies.append(pltpu.make_async_copy(maps, held, sems.at[F + 1]))
    copies.append(pltpu.make_async_copy(writers, held_writers, sems.at[F + 2]))
    for copy in copies:
        copy.start()
    copies[0].wait()
    both, send_hi = matrix[...], matrix[:32]
    dims = ((1,), (1,))
    for f in range(F):
        rows = slice(f * 256, f * 256 + 256)
        copies[1 + f].wait()
        cells_hi, cells_lo = halves(cells[rows])
        upper = dot(both, cells_hi, dims)
        shares = upper[:32] + dot(send_hi, cells_lo, dims) + upper[32:]
        to_low[:, rows] = shares[:16]
        to_high[:, rows] = shares[16:]
    copies[F + 1].wait()
    copies[F + 2].wait()


def fine_shares(values):
    return lift(values)


def coarse_shares(values):
    second = lift(lows(lift(values)))
    third = lift(lows(second))
    return second, third


class Lanes:
    def __init__(self):
        self.lane = lax.broadcasted_iota(jnp.int32, (8, LN), 1)
        self.second = self.lane % 2 == 0
        self.third = self.lane % 4 == 1
        self.ahead = [self.lane % 4 == (1 + i) % 4 for i in range(4)]

    @staticmethod
    def roll(x, by):
        return pltpu.roll(x, by % LN, 1) if by % LN else x

    def pack_second(self, rows):
        packed = []
        for i in range(0, len(rows), 2):
            odd = self.roll(rows[i + 1], 1) if i + 1 < len(rows) else rows[i]
            packed.append(jnp.where(self.second, rows[i], odd))
        return packed

    def pack_third(self, rows):
        packed = rows[0]
        for i in range(1, len(rows)):
            packed = jnp.where(self.ahead[i], self.roll(rows[i], i), packed)
        return packed


def send_rows(second, third, lanes):
    near_low = lanes.pack_second([second[i - 6] for i in range(6)]) + [lanes.pack_third([third[i - 4] for i in range(4)])]
    near_high = lanes.pack_second([second[8 + i] for i in range(5)]) + [lanes.pack_third([third[4 + i] for i in range(4)])]
    return near_low, near_high, lanes.pack_third([third[-6], third[-5]]), lanes.pack_third([third[8], third[9], third[10]])


def slots_of(row):
    shape = (TILES, TILES)
    wide = jnp.broadcast_to(row, shape)
    other = lax.broadcasted_iota(jnp.int32, shape, 0)
    tile = lax.broadcasted_iota(jnp.int32, shape, 1)
    zero = jnp.zeros(shape, jnp.float32)
    column = jnp.sum(jnp.where(other == tile, wide, zero), axis=1, keepdims=True)
    equal = jnp.where((wide == column) & (other < tile), zero + 1, zero)
    return row * 2 + jnp.sum(equal, axis=0, keepdims=True)


def own_y_kernel(writers, fields, maps, own, outbox, targets, zeros, sems):
    zeros[...] = jnp.zeros_like(zeros)
    copies = [pltpu.make_async_copy(zeros, outbox.at[pl.ds(i * 512, 512)], sems.at[i]) for i in range(4)]
    for copy in copies:
        copy.start()
    cells_hi, cells_lo = halves(fields[...])
    dims = ((1,), (0,))
    own_hi, own_lo = maps[:128], maps[128:256]
    own[...] = dot(cells_hi, own_hi, dims) + dot(cells_lo, own_hi, dims) + dot(cells_hi, own_lo, dims)
    targets[...] = slots_of(writers[...].astype(jnp.float32)).astype(jnp.int32)
    for copy in copies:
        copy.wait()


def share_z_kernel(
    own, maps, from_low, from_high, fine, coarse, to_low, to_high, to_low_far, to_high_far, work
):
    low_hi, low_lo = halves(from_high[...])
    high_hi, high_lo = halves(from_low[...])
    turned = ((0,), (0,))
    place_low, place_high = maps[256:272], maps[272:]
    work[...] = (
        own[...]
        + dot(low_hi, place_low, turned)
        + dot(low_lo, place_low, turned)
        + dot(high_hi, place_high, turned)
        + dot(high_lo, place_high, turned)
    )
    lanes = Lanes()
    for f in range(F):
        for half in (0, 8):
            rows = slice(half, half + 8)
            at = [f * 256 + z * 16 + half for z in range(NB)]
            done = fine_shares({z: work[at[z] : at[z] + 8, :LN] for z in range(NB)})
            for z in range(NB):
                fine[at[z] : at[z] + 8] = done[z]
            for i in range(4):
                to_low[f, i, rows] = done[i - 4]
            for i in range(3):
                to_high[f, i, rows] = done[16 + i]
            second, third = coarse_shares({z: work[at[z] : at[z] + 8, LN:] for z in range(NB)})
            for z in range(8):
                row = jnp.where(lanes.second, second[z], third[z // 2]) if z % 2 == 0 else second[z]
                coarse[f * 128 + z * 16 + half : f * 128 + z * 16 + half + 8] = row
            near_low, near_high, far_low, far_high = send_rows(second, third, lanes)
            for i in range(4):
                to_low[f, 4 + i, rows] = near_low[i]
                to_high[f, 3 + i, rows] = near_high[i]
            to_low_far[f, rows] = far_low
            to_high_far[f, rows] = far_high


def add_coarse(base, near_low, near_high, far_low, far_high, lanes):
    zero = jnp.zeros_like(base[0])
    extra = [zero] * 8
    for i in range(6):
        extra[2 + i] = extra[2 + i] + lanes.roll(near_low[i // 2], -(i % 2))
    for i in range(5):
        extra[i] = extra[i] + lanes.roll(near_high[i // 2], -(i % 2))
    near = near_low[3] + near_high[3]
    near = near + jnp.where(lanes.ahead[3], zero, far_high)
    third = [lanes.roll(near, -r) for r in range(4)]
    third[2] = third[2] + far_low
    third[3] = third[3] + lanes.roll(far_low, -1)
    rows = []
    for i in range(8):
        other = jnp.where(lanes.third, third[i // 2], zero) if i % 2 == 0 else zero
        rows.append(base[i] + jnp.where(lanes.second, extra[i], other))
    return rows


def fine_x_kernel(fine, from_high, from_low, own_fine, to_low, to_high, work):
    for f in range(F):
        at = f * 256
        work[at : at + 48] = fine[at : at + 48] + from_low[f, :3].reshape(48, LN)
        work[at + 48 : at + 192] = fine[at + 48 : at + 192]
        work[at + 192 : at + 256] = fine[at + 192 : at + 256] + from_high[f, :4].reshape(64, LN)
    for g in range(10):
        rows = slice(g * 8, g * 8 + 8)
        done = fine_shares({x: work[pl.ds(g * 128 + x, 8, stride=16), :] for x in range(NB)})
        for x in range(NB):
            own_fine[x, rows] = done[x]
        for i in range(4):
            to_low[i * 80 + g * 8 : i * 80 + g * 8 + 8] = done[i - 4]
        for i in range(3):
            to_high[i * 80 + g * 8 : i * 80 + g * 8 + 8] = done[16 + i]


def coarse_x_kernel(
    coarse, from_high, from_low, from_high_far, from_low_far, held_low, held_high,
    own_coarse, to_low, to_high, to_low_far, to_high_far, work_coarse,
):
    del held_low, held_high
    lanes = Lanes()
    for f in range(F):
        for half in (0, 8):
            rows = slice(half, half + 8)
            at = [f * 128 + z * 16 + half for z in range(8)]
            added = add_coarse(
                [coarse[at[z] : at[z] + 8] for z in range(8)],
                [from_high[f, 4 + i, rows] for i in range(4)],
                [from_low[f, 3 + i, rows] for i in range(4)],
                from_high_far[f, rows],
                from_low_far[f, rows],
                lanes,
            )
            for z in range(8):
                work_coarse[at[z] : at[z] + 8] = added[z]
    for g in range(5):
        rows = slice(g * 8, g * 8 + 8)
        second, third = coarse_shares({x: work_coarse[pl.ds(g * 128 + x, 8, stride=16), :] for x in range(NB)})
        for x in range(8):
            own_coarse[x, rows] = jnp.where(lanes.second, second[x], third[x // 2]) if x % 2 == 0 else second[x]
        near_low, near_high, far_low, far_high = send_rows(second, third, lanes)
        for i in range(4):
            to_low[320 + i * 40 + g * 8 : 320 + i * 40 + g * 8 + 8] = near_low[i]
            to_high[240 + i * 40 + g * 8 : 240 + i * 40 + g * 8 + 8] = near_high[i]
        to_low_far[rows] = far_low
        to_high_far[rows] = far_high


def tile_copies(targets, tiles, outbox, sems, first):
    copies = []
    for i in range(TILES // 2):
        t = 2 * i + first
        to = pl.multiple_of(targets[t] * 16, 16)
        copies.append(pltpu.make_async_copy(tiles.at[pl.ds(t * 16, 16)], outbox.at[pl.ds(to, 16)], sems.at[i]))
    return copies


def tiles_kernel(targets, fine, from_high, from_low, cleared, tiles, outbox, sems):
    del cleared
    for g in range(10):
        rows = slice(g * 8, g * 8 + 8)
        for x in range(NB):
            row = fine[x, rows]
            if x < 3:
                row = row + from_low[x * 80 + g * 8 : x * 80 + g * 8 + 8]
            if x >= 12:
                i = x - 12
                row = row + from_high[i * 80 + g * 8 : i * 80 + g * 8 + 8]
            tiles[pl.ds(g * 128 + x, 8, stride=16), :] = row
    copies = tile_copies(targets, tiles, outbox, sems, 1)
    for copy in copies:
        copy.start()
    for copy in copies:
        copy.wait()


def route_kernel(
    targets, tiles, coarse, from_high, from_low, from_high_far, from_low_far, filled,
    outbox, low_rows, spread, whole, sems,
):
    del filled
    copies = tile_copies(targets, whole, outbox, sems, 0)
    shape = (8, LN)
    lanes = Lanes()
    even_row = lax.broadcasted_iota(jnp.int32, shape, 0) % 2 == 0
    replaced = (lanes.lane % 4 == 0) & even_row
    merged = lanes.second & even_row
    for g in range(5):
        rows = slice(g * 8, g * 8 + 8)
        added = add_coarse(
            [coarse[x, rows] for x in range(8)],
            [from_high[320 + i * 40 + g * 8 : 320 + i * 40 + g * 8 + 8] for i in range(4)],
            [from_low[240 + i * 40 + g * 8 : 240 + i * 40 + g * 8 + 8] for i in range(4)],
            from_high_far[rows],
            from_low_far[rows],
            lanes,
        )
        for x in range(8):
            row = added[x]
            if x % 2 == 0:
                row = jnp.where(replaced, lanes.roll(row, -1), row)
            for odd in range(2):
                spread[pl.ds(g * 128 + 2 * x + odd, 8, stride=16), :] = row
        for z in range(0, NB, 2):
            t = g * NB + z
            for half in (0, 8):
                at = (g * 8 + z // 2) * 16 + half
                here = slice(t * 16 + half, t * 16 + half + 8)
                whole[here] = jnp.where(merged, spread[at : at + 8], tiles[here])
            copies[t // 2].start()
        low_rows[g * 8 : g * 8 + 8] = added[0]
        low_rows[40 + g * 8 : 40 + g * 8 + 8] = added[4]
    for copy in copies:
        copy.wait()


def pick_kernel(rows, low_band):
    picked = (LN, 16)
    pick = lax.broadcasted_iota(jnp.int32, picked, 0) == 8 * lax.broadcasted_iota(jnp.int32, picked, 1) + 1
    pick = jnp.where(pick, jnp.ones(picked, jnp.float32), jnp.zeros(picked, jnp.float32)).astype(jnp.bfloat16)
    upper, lower = halves(rows[...])
    rest = (rows[...] - upper.astype(jnp.float32) - lower.astype(jnp.float32)).astype(jnp.bfloat16)
    dims = ((1,), (0,))
    low_band[...] = dot(upper, pick, dims) + dot(lower, pick, dims) + dot(rest, pick, dims)


VM = pl.BlockSpec(memory_space=pltpu.VMEM)
SM = pl.BlockSpec(memory_space=pltpu.SMEM)
HB = pl.BlockSpec(memory_space=pltpu.HBM)


def f32(*shape):
    return jax.ShapeDtypeStruct(shape, jnp.float32)


def call(kernel, outs, ins, scratch=(), specs=None, out_specs=None, flops=1 << 20, grant=32 << 20, aliases=None):
    moved = sum(4 * int(np.prod(a.shape)) for a in list(outs) + list(ins))
    return pl.pallas_call(
        kernel,
        out_shape=list(outs),
        in_specs=specs or [VM] * len(ins),
        out_specs=out_specs or [VM] * len(outs),
        scratch_shapes=list(scratch),
        input_output_aliases=aliases or {},
        compiler_params=pltpu.CompilerParams(vmem_limit_bytes=grant),
        cost_estimate=pl.CostEstimate(flops=flops, bytes_accessed=moved, transcendentals=0),
    )(*ins)


def shift(array, axis, by):
    count = lax.axis_size(axis)
    return lax.ppermute(array, axis, [(i, (i + by) % count) for i in range(count)])


def coarse_matrix(length):
    level_four = lift_np(np.eye(length))
    level_five = lift_np(level_four[0::2])
    level_four[0::2] = level_five
    return level_four.astype(np.float32)


def body(fields, tile_writer):
    send, own, place = y_matrices()
    send = jnp.asarray(np.concatenate(split(send)))
    maps = jnp.asarray(np.concatenate([*split(own), place.astype(ml_dtypes.bfloat16)]))
    cells = fields.reshape(ROWS, LN)
    writers = tile_writer.reshape(1, TILES)

    to_low, to_high, cells, maps, writers = call(
        share_y_kernel,
        [f32(16, ROWS), f32(16, ROWS), f32(ROWS, LN)] + [jax.ShapeDtypeStruct(a.shape, a.dtype) for a in (maps, writers)],
        [pltpu.with_memory_space_constraint(a, pltpu.HBM) for a in (cells, send, maps, writers)],
        [pltpu.VMEM((64, LN), jnp.bfloat16), pltpu.SemaphoreType.DMA((F + 3,))],
        [HB, HB, HB, HB],
        grant=32 << 20,
    )
    own, outbox, targets = call(
        own_y_kernel,
        [f32(ROWS, 2 * LN), f32(2048, LN), jax.ShapeDtypeStruct((1, TILES), jnp.int32)],
        [writers, cells, maps],
        [pltpu.VMEM((512, LN), jnp.float32), pltpu.SemaphoreType.DMA((4,))],
        out_specs=[VM, HB, VM],
        flops=1 << 30,
    )
    from_high = shift(to_low, "gy", -1)
    from_low = shift(to_high, "gy", 1)

    fine, coarse, to_low, to_high, to_low_far, to_high_far = call(
        share_z_kernel,
        [f32(ROWS, LN), f32(ROWS // 2, LN), f32(F, 8, 16, LN), f32(F, 7, 16, LN), f32(F, 16, LN), f32(F, 16, LN)],
        [own, maps, from_low, from_high],
        [pltpu.VMEM((ROWS, 2 * LN), jnp.float32)],
    )
    from_high = shift(to_low, "gz", -1)
    from_low = shift(to_high, "gz", 1)
    from_high_far = shift(to_low_far, "gz", -2)
    from_low_far = shift(to_high_far, "gz", 2)

    fine, to_low, to_high = call(
        fine_x_kernel,
        [f32(16, 80, LN), f32(480, LN), f32(400, LN)],
        [fine, from_high, from_low],
        [pltpu.VMEM((ROWS, LN), jnp.float32)],
        flops=1 << 30,
    )
    coarse, to_low, to_high, to_low_far, to_high_far = call(
        coarse_x_kernel,
        [f32(8, 40, LN), f32(480, LN), f32(400, LN), f32(40, LN), f32(40, LN)],
        [coarse, from_high, from_low, from_high_far, from_low_far, to_low, to_high],
        [pltpu.VMEM((ROWS // 2, LN), jnp.float32)],
        aliases={5: 1, 6: 2},
    )
    from_high = shift(to_low, "gx", -1)
    from_low = shift(to_high, "gx", 1)
    from_high_far = shift(to_low_far, "gx", -2)
    from_low_far = shift(to_high_far, "gx", 2)

    targets = targets.reshape(TILES)
    tiles, outbox = call(
        tiles_kernel,
        [f32(ROWS, LN), f32(2048, LN)],
        [targets, fine, from_high, from_low, outbox],
        [pltpu.SemaphoreType.DMA((TILES // 2,))],
        [SM, VM, VM, VM, HB],
        [VM, HB],
        flops=1 << 30,
        aliases={4: 1},
    )
    outbox, low_rows = call(
        route_kernel,
        [f32(2048, LN), f32(80, LN)],
        [targets, tiles, coarse, from_high, from_low, from_high_far, from_low_far, outbox],
        [pltpu.VMEM((640, LN), jnp.float32), pltpu.VMEM((ROWS, LN), jnp.float32), pltpu.SemaphoreType.DMA((TILES // 2,))],
        [SM] + [VM] * 6 + [HB],
        [HB, VM],
        aliases={7: 0},
    )
    inbox = lax.all_to_all(outbox.reshape(64, 32, LN), ("gx", "gy"), split_axis=0, concat_axis=0, tiled=True)

    (low_band,) = call(pick_kernel, [f32(80, 16)], [low_rows])
    band = low_band.reshape(2, F, 8, 16)[:, :, ::4].transpose(2, 1, 0, 3).reshape(2, F * 32)
    band = lax.all_gather(band, "gz", axis=0, tiled=True)
    turn = jnp.asarray(coarse_matrix(band.shape[0]))
    bands = jnp.dot(turn, band, precision=lax.Precision.HIGHEST)
    bands = bands.reshape(-1, F, 2, 16).transpose(1, 0, 2, 3)
    return (bands, inbox.reshape(128, 2048))


def solution(mesh):
    return jax.shard_map(
        body,
        mesh=mesh,
        in_specs=(P(None, "gz", "gx", "gy"), P("gx", "gy", "gz", None)),
        out_specs=(P(None, None, "gx", "gy"), P(("gx", "gy"), "gz")),
        check_vma=False,
    )
```

```python
import jax
import jax.numpy as jnp
import ml_dtypes
import numpy as np
from jax import lax
from jax.experimental import pallas as pl
from jax.experimental.pallas import tpu as pltpu
from jax.sharding import PartitionSpec as P

PREDICT_ONE = -1.586134342059924
UPDATE_ONE = -0.052980118572961
PREDICT_TWO = 0.882911075530934
UPDATE_TWO = 0.443506852043971
LOW_SCALE = 1.0 / 1.149604398860241
HIGH_SCALE = 1.149604398860241

F = 5
NB = 16
LN = 128
ROWS = F * NB * NB
TILES = F * NB

LOW_SIDE = (4, 6, 6)
HIGH_SIDE = (3, 5, 7)


def lift_np(values):
    low = values[0::2].copy()
    high = values[1::2].copy()
    high += PREDICT_ONE * (low + np.roll(low, -1, 0))
    low += UPDATE_ONE * (np.roll(high, 1, 0) + high)
    high += PREDICT_TWO * (low + np.roll(low, -1, 0))
    low += UPDATE_TWO * (np.roll(high, 1, 0) + high)
    joined = np.empty_like(values)
    joined[0::2] = low * LOW_SCALE
    joined[1::2] = high * HIGH_SCALE
    return joined


def split(matrix):
    matrix = np.asarray(matrix, np.float32)
    upper = matrix.astype(ml_dtypes.bfloat16)
    lower = (matrix - upper.astype(np.float32)).astype(ml_dtypes.bfloat16)
    return upper, lower


def y_matrices():
    total, start = 8 * LN, 4 * LN
    level = np.eye(total)
    maps = []
    for _ in range(3):
        level = lift_np(level)
        maps.append(level)
        level = level[0::2]
    own = np.zeros((LN, 2 * LN))
    send = np.zeros((32, LN))
    place = np.zeros((32, 2 * LN))
    columns = [lambda j: j, lambda j: LN + 2 * j, lambda j: LN + 4 * j + 1]
    at_low, at_high = 0, 16
    for depth in range(3):
        count = LN >> depth
        first = start >> depth
        block = maps[depth][:, start : start + LN]
        low, high = LOW_SIDE[depth], HIGH_SIDE[depth]
        assert not block[: first - low].any() and not block[first + count + high :].any()
        for j in range(count):
            own[:, columns[depth](j)] = block[first + j]
        for j in range(low):
            send[at_low] = block[first - low + j]
            place[at_low, columns[depth](count - low + j)] = 1
            at_low += 1
        for j in range(high):
            send[at_high] = block[first + count + j]
            place[at_high, columns[depth](j)] = 1
            at_high += 1
    return send, own, place


def lift(values):
    low = {i // 2: v for i, v in values.items() if i % 2 == 0}
    high = {i // 2: v for i, v in values.items() if i % 2 != 0}

    def add(target, source, factor, offsets):
        span = range(min(source) - 1, max(source) + 2)
        result = dict(target)
        for i in span:
            terms = [source[i + o] for o in offsets if i + o in source]
            if terms:
                step = factor * (terms[0] + terms[1] if len(terms) == 2 else terms[0])
                result[i] = result[i] + step if i in result else step
        return result

    high = add(high, low, PREDICT_ONE, (0, 1))
    low = add(low, high, UPDATE_ONE, (-1, 0))
    high = add(high, low, PREDICT_TWO, (0, 1))
    low = add(low, high, UPDATE_TWO, (-1, 0))
    joined = {2 * i: v * LOW_SCALE for i, v in low.items()}
    joined.update({2 * i + 1: v * HIGH_SCALE for i, v in high.items()})
    return joined


def lows(values):
    return {i // 2: v for i, v in values.items() if i % 2 == 0}


def dot(a, b, dims):
    return lax.dot_general(a, b, (dims, ((), ())), preferred_element_type=jnp.float32)


def halves(x):
    upper = x.astype(jnp.bfloat16)
    return upper, (x - upper.astype(jnp.float32)).astype(jnp.bfloat16)


def share_y_kernel(fields, send, maps, writers, to_low, to_high, cells, held, held_writers, matrix, sems):
    copies = [pltpu.make_async_copy(send, matrix, sems.at[F])]
    for f in range(F):
        rows = pl.ds(f * 256, 256)
        copies.append(pltpu.make_async_copy(fields.at[rows], cells.at[rows], sems.at[f]))
    copies.append(pltpu.make_async_copy(maps, held, sems.at[F + 1]))
    copies.append(pltpu.make_async_copy(writers, held_writers, sems.at[F + 2]))
    for copy in copies:
        copy.start()
    copies[0].wait()
    both, send_hi = matrix[...], matrix[:32]
    dims = ((1,), (1,))
    for f in range(F):
        rows = slice(f * 256, f * 256 + 256)
        copies[1 + f].wait()
        cells_hi, cells_lo = halves(cells[rows])
        upper = dot(both, cells_hi, dims)
        shares = upper[:32] + dot(send_hi, cells_lo, dims) + upper[32:]
        to_low[:, rows] = shares[:16]
        to_high[:, rows] = shares[16:]
    copies[F + 1].wait()
    copies[F + 2].wait()


def fine_shares(values):
    return lift(values)


def coarse_shares(values):
    second = lift(lows(lift(values)))
    third = lift(lows(second))
    return second, third


class Lanes:
    def __init__(self):
        self.lane = lax.broadcasted_iota(jnp.int32, (8, LN), 1)
        self.second = self.lane % 2 == 0
        self.third = self.lane % 4 == 1
        self.ahead = [self.lane % 4 == (1 + i) % 4 for i in range(4)]

    @staticmethod
    def roll(x, by):
        return pltpu.roll(x, by % LN, 1) if by % LN else x

    def pack_second(self, rows):
        packed = []
        for i in range(0, len(rows), 2):
            odd = self.roll(rows[i + 1], 1) if i + 1 < len(rows) else rows[i]
            packed.append(jnp.where(self.second, rows[i], odd))
        return packed

    def pack_third(self, rows):
        packed = rows[0]
        for i in range(1, len(rows)):
            packed = jnp.where(self.ahead[i], self.roll(rows[i], i), packed)
        return packed


def send_rows(second, third, lanes):
    near_low = lanes.pack_second([second[i - 6] for i in range(6)]) + [lanes.pack_third([third[i - 4] for i in range(4)])]
    near_high = lanes.pack_second([second[8 + i] for i in range(5)]) + [lanes.pack_third([third[4 + i] for i in range(4)])]
    return near_low, near_high, lanes.pack_third([third[-6], third[-5]]), lanes.pack_third([third[8], third[9], third[10]])


def slots_of(row):
    shape = (TILES, TILES)
    wide = jnp.broadcast_to(row, shape)
    other = lax.broadcasted_iota(jnp.int32, shape, 0)
    tile = lax.broadcasted_iota(jnp.int32, shape, 1)
    zero = jnp.zeros(shape, jnp.float32)
    column = jnp.sum(jnp.where(other == tile, wide, zero), axis=1, keepdims=True)
    equal = jnp.where((wide == column) & (other < tile), zero + 1, zero)
    return row * 2 + jnp.sum(equal, axis=0, keepdims=True)


def own_y_kernel(writers, fields, maps, own, targets):
    cells_hi, cells_lo = halves(fields[...])
    dims = ((1,), (0,))
    own_hi, own_lo = maps[:128], maps[128:256]
    own[...] = dot(cells_hi, own_hi, dims) + dot(cells_lo, own_hi, dims) + dot(cells_hi, own_lo, dims)
    targets[...] = slots_of(writers[...].astype(jnp.float32)).astype(jnp.int32)


def share_z_kernel(
    own, maps, from_low, from_high, fine, coarse, to_low, to_high, to_low_far, to_high_far, work
):
    low_hi, low_lo = halves(from_high[...])
    high_hi, high_lo = halves(from_low[...])
    turned = ((0,), (0,))
    place_low, place_high = maps[256:272], maps[272:]
    work[...] = (
        own[...]
        + dot(low_hi, place_low, turned)
        + dot(low_lo, place_low, turned)
        + dot(high_hi, place_high, turned)
        + dot(high_lo, place_high, turned)
    )
    lanes = Lanes()
    for f in range(F):
        for half in (0, 8):
            rows = slice(half, half + 8)
            at = [f * 256 + z * 16 + half for z in range(NB)]
            done = fine_shares({z: work[at[z] : at[z] + 8, :LN] for z in range(NB)})
            for z in range(NB):
                fine[at[z] : at[z] + 8] = done[z]
            for i in range(4):
                to_low[f, i, rows] = done[i - 4]
            for i in range(3):
                to_high[f, i, rows] = done[16 + i]
            second, third = coarse_shares({z: work[at[z] : at[z] + 8, LN:] for z in range(NB)})
            for z in range(8):
                row = jnp.where(lanes.second, second[z], third[z // 2]) if z % 2 == 0 else second[z]
                coarse[f * 128 + z * 16 + half : f * 128 + z * 16 + half + 8] = row
            near_low, near_high, far_low, far_high = send_rows(second, third, lanes)
            for i in range(4):
                to_low[f, 4 + i, rows] = near_low[i]
                to_high[f, 3 + i, rows] = near_high[i]
            to_low_far[f, rows] = far_low
            to_high_far[f, rows] = far_high


def add_coarse(base, near_low, near_high, far_low, far_high, lanes):
    zero = jnp.zeros_like(base[0])
    extra = [zero] * 8
    for i in range(6):
        extra[2 + i] = extra[2 + i] + lanes.roll(near_low[i // 2], -(i % 2))
    for i in range(5):
        extra[i] = extra[i] + lanes.roll(near_high[i // 2], -(i % 2))
    near = near_low[3] + near_high[3]
    near = near + jnp.where(lanes.ahead[3], zero, far_high)
    third = [lanes.roll(near, -r) for r in range(4)]
    third[2] = third[2] + far_low
    third[3] = third[3] + lanes.roll(far_low, -1)
    rows = []
    for i in range(8):
        other = jnp.where(lanes.third, third[i // 2], zero) if i % 2 == 0 else zero
        rows.append(base[i] + jnp.where(lanes.second, extra[i], other))
    return rows


def fine_x_kernel(fine, from_high, from_low, own_fine, to_low, to_high, work):
    for f in range(F):
        at = f * 256
        work[at : at + 48] = fine[at : at + 48] + from_low[f, :3].reshape(48, LN)
        work[at + 48 : at + 192] = fine[at + 48 : at + 192]
        work[at + 192 : at + 256] = fine[at + 192 : at + 256] + from_high[f, :4].reshape(64, LN)
    for g in range(10):
        rows = slice(g * 8, g * 8 + 8)
        done = fine_shares({x: work[pl.ds(g * 128 + x, 8, stride=16), :] for x in range(NB)})
        for x in range(NB):
            own_fine[x, rows] = done[x]
        for i in range(4):
            to_low[i * 80 + g * 8 : i * 80 + g * 8 + 8] = done[i - 4]
        for i in range(3):
            to_high[i * 80 + g * 8 : i * 80 + g * 8 + 8] = done[16 + i]


def coarse_x_kernel(
    coarse, from_high, from_low, from_high_far, from_low_far, held_low, held_high,
    own_coarse, to_low, to_high, to_low_far, to_high_far, work_coarse,
):
    del held_low, held_high
    lanes = Lanes()
    for f in range(F):
        for half in (0, 8):
            rows = slice(half, half + 8)
            at = [f * 128 + z * 16 + half for z in range(8)]
            added = add_coarse(
                [coarse[at[z] : at[z] + 8] for z in range(8)],
                [from_high[f, 4 + i, rows] for i in range(4)],
                [from_low[f, 3 + i, rows] for i in range(4)],
                from_high_far[f, rows],
                from_low_far[f, rows],
                lanes,
            )
            for z in range(8):
                work_coarse[at[z] : at[z] + 8] = added[z]
    for g in range(5):
        rows = slice(g * 8, g * 8 + 8)
        second, third = coarse_shares({x: work_coarse[pl.ds(g * 128 + x, 8, stride=16), :] for x in range(NB)})
        for x in range(8):
            own_coarse[x, rows] = jnp.where(lanes.second, second[x], third[x // 2]) if x % 2 == 0 else second[x]
        near_low, near_high, far_low, far_high = send_rows(second, third, lanes)
        for i in range(4):
            to_low[320 + i * 40 + g * 8 : 320 + i * 40 + g * 8 + 8] = near_low[i]
            to_high[240 + i * 40 + g * 8 : 240 + i * 40 + g * 8 + 8] = near_high[i]
        to_low_far[rows] = far_low
        to_high_far[rows] = far_high


def tiles_kernel(targets, fine, from_high, from_low, tiles, outbox):
    outbox[...] = jnp.zeros_like(outbox)
    for g in range(10):
        rows = slice(g * 8, g * 8 + 8)
        for x in range(NB):
            row = fine[x, rows]
            if x < 3:
                row = row + from_low[x * 80 + g * 8 : x * 80 + g * 8 + 8]
            if x >= 12:
                i = x - 12
                row = row + from_high[i * 80 + g * 8 : i * 80 + g * 8 + 8]
            tiles[pl.ds(g * 128 + x, 8, stride=16), :] = row
    for t in range(1, TILES, 2):
        to = pl.multiple_of(targets[t] * 16, 16)
        outbox[pl.ds(to, 16), :] = tiles[t * 16 : t * 16 + 16]


def route_kernel(
    targets, tiles, coarse, from_high, from_low, from_high_far, from_low_far, filled,
    outbox, filling, low_rows, spread, sems,
):
    del filled
    shape = (8, LN)
    lanes = Lanes()
    even_row = lax.broadcasted_iota(jnp.int32, shape, 0) % 2 == 0
    replaced = (lanes.lane % 4 == 0) & even_row
    merged = lanes.second & even_row
    for g in range(5):
        rows = slice(g * 8, g * 8 + 8)
        added = add_coarse(
            [coarse[x, rows] for x in range(8)],
            [from_high[320 + i * 40 + g * 8 : 320 + i * 40 + g * 8 + 8] for i in range(4)],
            [from_low[240 + i * 40 + g * 8 : 240 + i * 40 + g * 8 + 8] for i in range(4)],
            from_high_far[rows],
            from_low_far[rows],
            lanes,
        )
        for x in range(8):
            row = added[x]
            if x % 2 == 0:
                row = jnp.where(replaced, lanes.roll(row, -1), row)
            for odd in range(2):
                spread[pl.ds(g * 128 + 2 * x + odd, 8, stride=16), :] = row
        for z in range(0, NB, 2):
            t = g * NB + z
            to = pl.multiple_of(targets[t] * 16, 16)
            for half in (0, 8):
                at = (g * 8 + z // 2) * 16 + half
                row = jnp.where(merged, spread[at : at + 8], tiles[t * 16 + half : t * 16 + half + 8])
                filling[pl.ds(to + half, 8), :] = row
        low_rows[g * 8 : g * 8 + 8] = added[0]
        low_rows[40 + g * 8 : 40 + g * 8 + 8] = added[4]
    copies = []
    for i in range(4):
        rows = pl.ds(i * 512, 512)
        copies.append(pltpu.make_async_copy(filling.at[rows], outbox.at[rows], sems.at[i]))
    for copy in copies:
        copy.start()
    for copy in copies:
        copy.wait()


def pick_kernel(rows, low_band):
    picked = (LN, 16)
    pick = lax.broadcasted_iota(jnp.int32, picked, 0) == 8 * lax.broadcasted_iota(jnp.int32, picked, 1) + 1
    pick = jnp.where(pick, jnp.ones(picked, jnp.float32), jnp.zeros(picked, jnp.float32)).astype(jnp.bfloat16)
    upper, lower = halves(rows[...])
    rest = (rows[...] - upper.astype(jnp.float32) - lower.astype(jnp.float32)).astype(jnp.bfloat16)
    dims = ((1,), (0,))
    low_band[...] = dot(upper, pick, dims) + dot(lower, pick, dims) + dot(rest, pick, dims)


VM = pl.BlockSpec(memory_space=pltpu.VMEM)
SM = pl.BlockSpec(memory_space=pltpu.SMEM)
HB = pl.BlockSpec(memory_space=pltpu.HBM)


def f32(*shape):
    return jax.ShapeDtypeStruct(shape, jnp.float32)


def call(kernel, outs, ins, scratch=(), specs=None, out_specs=None, flops=1 << 20, grant=32 << 20, aliases=None):
    moved = sum(4 * int(np.prod(a.shape)) for a in list(outs) + list(ins))
    return pl.pallas_call(
        kernel,
        out_shape=list(outs),
        in_specs=specs or [VM] * len(ins),
        out_specs=out_specs or [VM] * len(outs),
        scratch_shapes=list(scratch),
        input_output_aliases=aliases or {},
        compiler_params=pltpu.CompilerParams(vmem_limit_bytes=grant),
        cost_estimate=pl.CostEstimate(flops=flops, bytes_accessed=moved, transcendentals=0),
    )(*ins)


def shift(array, axis, by):
    count = lax.axis_size(axis)
    return lax.ppermute(array, axis, [(i, (i + by) % count) for i in range(count)])


def coarse_matrix(length):
    level_four = lift_np(np.eye(length))
    level_five = lift_np(level_four[0::2])
    level_four[0::2] = level_five
    return level_four.astype(np.float32)


def body(fields, tile_writer):
    send, own, place = y_matrices()
    send = jnp.asarray(np.concatenate(split(send)))
    maps = jnp.asarray(np.concatenate([*split(own), place.astype(ml_dtypes.bfloat16)]))
    cells = fields.reshape(ROWS, LN)
    writers = tile_writer.reshape(1, TILES)

    to_low, to_high, cells, maps, writers = call(
        share_y_kernel,
        [f32(16, ROWS), f32(16, ROWS), f32(ROWS, LN)] + [jax.ShapeDtypeStruct(a.shape, a.dtype) for a in (maps, writers)],
        [pltpu.with_memory_space_constraint(a, pltpu.HBM) for a in (cells, send, maps, writers)],
        [pltpu.VMEM((64, LN), jnp.bfloat16), pltpu.SemaphoreType.DMA((F + 3,))],
        [HB, HB, HB, HB],
        grant=32 << 20,
    )
    own, targets = call(
        own_y_kernel,
        [f32(ROWS, 2 * LN), jax.ShapeDtypeStruct((1, TILES), jnp.int32)],
        [writers, cells, maps],
        flops=1 << 30,
    )
    from_high = shift(to_low, "gy", -1)
    from_low = shift(to_high, "gy", 1)

    fine, coarse, to_low, to_high, to_low_far, to_high_far = call(
        share_z_kernel,
        [f32(ROWS, LN), f32(ROWS // 2, LN), f32(F, 8, 16, LN), f32(F, 7, 16, LN), f32(F, 16, LN), f32(F, 16, LN)],
        [own, maps, from_low, from_high],
        [pltpu.VMEM((ROWS, 2 * LN), jnp.float32)],
    )
    from_high = shift(to_low, "gz", -1)
    from_low = shift(to_high, "gz", 1)
    from_high_far = shift(to_low_far, "gz", -2)
    from_low_far = shift(to_high_far, "gz", 2)

    fine, to_low, to_high = call(
        fine_x_kernel,
        [f32(16, 80, LN), f32(480, LN), f32(400, LN)],
        [fine, from_high, from_low],
        [pltpu.VMEM((ROWS, LN), jnp.float32)],
        flops=1 << 30,
    )
    coarse, to_low, to_high, to_low_far, to_high_far = call(
        coarse_x_kernel,
        [f32(8, 40, LN), f32(480, LN), f32(400, LN), f32(40, LN), f32(40, LN)],
        [coarse, from_high, from_low, from_high_far, from_low_far, to_low, to_high],
        [pltpu.VMEM((ROWS // 2, LN), jnp.float32)],
        aliases={5: 1, 6: 2},
    )
    from_high = shift(to_low, "gx", -1)
    from_low = shift(to_high, "gx", 1)
    from_high_far = shift(to_low_far, "gx", -2)
    from_low_far = shift(to_high_far, "gx", 2)

    targets = targets.reshape(TILES)
    tiles, filling = call(
        tiles_kernel,
        [f32(ROWS, LN), f32(2048, LN)],
        [targets, fine, from_high, from_low],
        specs=[SM, VM, VM, VM],
        flops=1 << 30,
    )
    outbox, _, low_rows = call(
        route_kernel,
        [f32(2048, LN), f32(2048, LN), f32(80, LN)],
        [targets, tiles, coarse, from_high, from_low, from_high_far, from_low_far, filling],
        [pltpu.VMEM((640, LN), jnp.float32), pltpu.SemaphoreType.DMA((4,))],
        [SM] + [VM] * 7,
        [HB, VM, VM],
        aliases={7: 1},
    )
    inbox = lax.all_to_all(outbox.reshape(64, 32, LN), ("gx", "gy"), split_axis=0, concat_axis=0, tiled=True)

    (low_band,) = call(pick_kernel, [f32(80, 16)], [low_rows])
    band = low_band.reshape(2, F, 8, 16)[:, :, ::4].transpose(2, 1, 0, 3).reshape(2, F * 32)
    band = lax.all_gather(band, "gz", axis=0, tiled=True)
    turn = jnp.asarray(coarse_matrix(band.shape[0]))
    bands = jnp.dot(turn, band, precision=lax.Precision.HIGHEST)
    bands = bands.reshape(-1, F, 2, 16).transpose(1, 0, 2, 3)
    return (bands, inbox.reshape(128, 2048))


def solution(mesh):
    return jax.shard_map(
        body,
        mesh=mesh,
        in_specs=(P(None, "gz", "gx", "gy"), P("gx", "gy", "gz", None)),
        out_specs=(P(None, None, "gx", "gy"), P(("gx", "gy"), "gz")),
        check_vma=False,
    )
```

```python
import jax
import jax.numpy as jnp
import ml_dtypes
import numpy as np
from jax import lax
from jax.experimental import pallas as pl
from jax.experimental.pallas import tpu as pltpu
from jax.sharding import PartitionSpec as P

PREDICT_ONE = -1.586134342059924
UPDATE_ONE = -0.052980118572961
PREDICT_TWO = 0.882911075530934
UPDATE_TWO = 0.443506852043971
LOW_SCALE = 1.0 / 1.149604398860241
HIGH_SCALE = 1.149604398860241

F = 5
NB = 16
LN = 128
ROWS = F * NB * NB
TILES = F * NB

LOW_SIDE = (4, 6, 6)
HIGH_SIDE = (3, 5, 7)


def lift_np(values):
    low = values[0::2].copy()
    high = values[1::2].copy()
    high += PREDICT_ONE * (low + np.roll(low, -1, 0))
    low += UPDATE_ONE * (np.roll(high, 1, 0) + high)
    high += PREDICT_TWO * (low + np.roll(low, -1, 0))
    low += UPDATE_TWO * (np.roll(high, 1, 0) + high)
    joined = np.empty_like(values)
    joined[0::2] = low * LOW_SCALE
    joined[1::2] = high * HIGH_SCALE
    return joined


def split(matrix):
    matrix = np.asarray(matrix, np.float32)
    upper = matrix.astype(ml_dtypes.bfloat16)
    lower = (matrix - upper.astype(np.float32)).astype(ml_dtypes.bfloat16)
    return upper, lower


def y_matrices():
    total, start = 8 * LN, 4 * LN
    level = np.eye(total)
    maps = []
    for _ in range(3):
        level = lift_np(level)
        maps.append(level)
        level = level[0::2]
    own = np.zeros((LN, 2 * LN))
    send = np.zeros((32, LN))
    place = np.zeros((32, 2 * LN))
    columns = [lambda j: j, lambda j: LN + 2 * j, lambda j: LN + 4 * j + 1]
    at_low, at_high = 0, 16
    for depth in range(3):
        count = LN >> depth
        first = start >> depth
        block = maps[depth][:, start : start + LN]
        low, high = LOW_SIDE[depth], HIGH_SIDE[depth]
        assert not block[: first - low].any() and not block[first + count + high :].any()
        for j in range(count):
            own[:, columns[depth](j)] = block[first + j]
        for j in range(low):
            send[at_low] = block[first - low + j]
            place[at_low, columns[depth](count - low + j)] = 1
            at_low += 1
        for j in range(high):
            send[at_high] = block[first + count + j]
            place[at_high, columns[depth](j)] = 1
            at_high += 1
    return send, own, place


def lift(values):
    low = {i // 2: v for i, v in values.items() if i % 2 == 0}
    high = {i // 2: v for i, v in values.items() if i % 2 != 0}

    def add(target, source, factor, offsets):
        span = range(min(source) - 1, max(source) + 2)
        result = dict(target)
        for i in span:
            terms = [source[i + o] for o in offsets if i + o in source]
            if terms:
                step = factor * (terms[0] + terms[1] if len(terms) == 2 else terms[0])
                result[i] = result[i] + step if i in result else step
        return result

    high = add(high, low, PREDICT_ONE, (0, 1))
    low = add(low, high, UPDATE_ONE, (-1, 0))
    high = add(high, low, PREDICT_TWO, (0, 1))
    low = add(low, high, UPDATE_TWO, (-1, 0))
    joined = {2 * i: v * LOW_SCALE for i, v in low.items()}
    joined.update({2 * i + 1: v * HIGH_SCALE for i, v in high.items()})
    return joined


def lows(values):
    return {i // 2: v for i, v in values.items() if i % 2 == 0}


def dot(a, b, dims):
    return lax.dot_general(a, b, (dims, ((), ())), preferred_element_type=jnp.float32)


def halves(x):
    upper = x.astype(jnp.bfloat16)
    return upper, (x - upper.astype(jnp.float32)).astype(jnp.bfloat16)


def share_y_kernel(fields, send, maps, writers, to_low, to_high, cells, held, held_writers, matrix, sems):
    copies = [pltpu.make_async_copy(send, matrix, sems.at[F])]
    for f in range(F):
        rows = pl.ds(f * 256, 256)
        copies.append(pltpu.make_async_copy(fields.at[rows], cells.at[rows], sems.at[f]))
    copies.append(pltpu.make_async_copy(maps, held, sems.at[F + 1]))
    copies.append(pltpu.make_async_copy(writers, held_writers, sems.at[F + 2]))
    for copy in copies:
        copy.start()
    copies[0].wait()
    both, send_hi = matrix[...], matrix[:32]
    dims = ((1,), (1,))
    for f in range(F):
        rows = slice(f * 256, f * 256 + 256)
        copies[1 + f].wait()
        cells_hi, cells_lo = halves(cells[rows])
        upper = dot(both, cells_hi, dims)
        shares = upper[:32] + dot(send_hi, cells_lo, dims) + upper[32:]
        to_low[:, rows] = shares[:16]
        to_high[:, rows] = shares[16:]
    copies[F + 1].wait()
    copies[F + 2].wait()


def fine_shares(values):
    return lift(values)


def coarse_shares(values):
    second = lift(lows(lift(values)))
    third = lift(lows(second))
    return second, third


class Lanes:
    def __init__(self):
        self.lane = lax.broadcasted_iota(jnp.int32, (8, LN), 1)
        self.second = self.lane % 2 == 0
        self.third = self.lane % 4 == 1
        self.ahead = [self.lane % 4 == (1 + i) % 4 for i in range(4)]

    @staticmethod
    def roll(x, by):
        return pltpu.roll(x, by % LN, 1) if by % LN else x

    def pack_second(self, rows):
        packed = []
        for i in range(0, len(rows), 2):
            odd = self.roll(rows[i + 1], 1) if i + 1 < len(rows) else rows[i]
            packed.append(jnp.where(self.second, rows[i], odd))
        return packed

    def pack_third(self, rows):
        packed = rows[0]
        for i in range(1, len(rows)):
            packed = jnp.where(self.ahead[i], self.roll(rows[i], i), packed)
        return packed


def send_rows(second, third, lanes):
    near_low = lanes.pack_second([second[i - 6] for i in range(6)]) + [lanes.pack_third([third[i - 4] for i in range(4)])]
    near_high = lanes.pack_second([second[8 + i] for i in range(5)]) + [lanes.pack_third([third[4 + i] for i in range(4)])]
    return near_low, near_high, lanes.pack_third([third[-6], third[-5]]), lanes.pack_third([third[8], third[9], third[10]])


def slots_of(row):
    shape = (TILES, TILES)
    wide = jnp.broadcast_to(row, shape)
    other = lax.broadcasted_iota(jnp.int32, shape, 0)
    tile = lax.broadcasted_iota(jnp.int32, shape, 1)
    zero = jnp.zeros(shape, jnp.float32)
    column = jnp.sum(jnp.where(other == tile, wide, zero), axis=1, keepdims=True)
    equal = jnp.where((wide == column) & (other < tile), zero + 1, zero)
    return row * 2 + jnp.sum(equal, axis=0, keepdims=True)


def own_y_kernel(writers, fields, maps, own, targets):
    cells_hi, cells_lo = halves(fields[...])
    dims = ((1,), (0,))
    own_hi, own_lo = maps[:128], maps[128:256]
    own[...] = dot(cells_hi, own_hi, dims) + dot(cells_lo, own_hi, dims) + dot(cells_hi, own_lo, dims)
    targets[...] = slots_of(writers[...].astype(jnp.float32)).astype(jnp.int32)


def share_z_kernel(
    own, maps, from_low, from_high, fine, coarse, to_low, to_high, to_low_far, to_high_far, work
):
    low_hi, low_lo = halves(from_high[...])
    high_hi, high_lo = halves(from_low[...])
    turned = ((0,), (0,))
    place_low, place_high = maps[256:272], maps[272:]
    work[...] = (
        own[...]
        + dot(low_hi, place_low, turned)
        + dot(low_lo, place_low, turned)
        + dot(high_hi, place_high, turned)
        + dot(high_lo, place_high, turned)
    )
    lanes = Lanes()
    for f in range(F):
        for half in (0, 8):
            rows = slice(half, half + 8)
            at = [f * 256 + z * 16 + half for z in range(NB)]
            done = fine_shares({z: work[at[z] : at[z] + 8, :LN] for z in range(NB)})
            for z in range(NB):
                fine[at[z] : at[z] + 8] = done[z]
            for i in range(4):
                to_low[f, i, rows] = done[i - 4]
            for i in range(3):
                to_high[f, i, rows] = done[16 + i]
            second, third = coarse_shares({z: work[at[z] : at[z] + 8, LN:] for z in range(NB)})
            for z in range(8):
                row = jnp.where(lanes.second, second[z], third[z // 2]) if z % 2 == 0 else second[z]
                coarse[f * 128 + z * 16 + half : f * 128 + z * 16 + half + 8] = row
            near_low, near_high, far_low, far_high = send_rows(second, third, lanes)
            for i in range(4):
                to_low[f, 4 + i, rows] = near_low[i]
                to_high[f, 3 + i, rows] = near_high[i]
            to_low_far[f, rows] = far_low
            to_high_far[f, rows] = far_high


def add_coarse(base, near_low, near_high, far_low, far_high, lanes):
    zero = jnp.zeros_like(base[0])
    extra = [zero] * 8
    for i in range(6):
        extra[2 + i] = extra[2 + i] + lanes.roll(near_low[i // 2], -(i % 2))
    for i in range(5):
        extra[i] = extra[i] + lanes.roll(near_high[i // 2], -(i % 2))
    near = near_low[3] + near_high[3]
    near = near + jnp.where(lanes.ahead[3], zero, far_high)
    third = [lanes.roll(near, -r) for r in range(4)]
    third[2] = third[2] + far_low
    third[3] = third[3] + lanes.roll(far_low, -1)
    rows = []
    for i in range(8):
        other = jnp.where(lanes.third, third[i // 2], zero) if i % 2 == 0 else zero
        rows.append(base[i] + jnp.where(lanes.second, extra[i], other))
    return rows


def fine_x_kernel(fine, from_high, from_low, own_fine, to_low, to_high, work):
    for f in range(F):
        at = f * 256
        work[at : at + 48] = fine[at : at + 48] + from_low[f, :3].reshape(48, LN)
        work[at + 48 : at + 192] = fine[at + 48 : at + 192]
        work[at + 192 : at + 256] = fine[at + 192 : at + 256] + from_high[f, :4].reshape(64, LN)
    for g in range(10):
        rows = slice(g * 8, g * 8 + 8)
        done = fine_shares({x: work[pl.ds(g * 128 + x, 8, stride=16), :] for x in range(NB)})
        for x in range(NB):
            own_fine[x, rows] = done[x]
        for i in range(4):
            to_low[i * 80 + g * 8 : i * 80 + g * 8 + 8] = done[i - 4]
        for i in range(3):
            to_high[i * 80 + g * 8 : i * 80 + g * 8 + 8] = done[16 + i]


def coarse_x_kernel(
    coarse, from_high, from_low, from_high_far, from_low_far, held_low, held_high,
    own_coarse, to_low, to_high, to_low_far, to_high_far, work_coarse,
):
    del held_low, held_high
    lanes = Lanes()
    for f in range(F):
        for half in (0, 8):
            rows = slice(half, half + 8)
            at = [f * 128 + z * 16 + half for z in range(8)]
            added = add_coarse(
                [coarse[at[z] : at[z] + 8] for z in range(8)],
                [from_high[f, 4 + i, rows] for i in range(4)],
                [from_low[f, 3 + i, rows] for i in range(4)],
                from_high_far[f, rows],
                from_low_far[f, rows],
                lanes,
            )
            for z in range(8):
                work_coarse[at[z] : at[z] + 8] = added[z]
    for g in range(5):
        rows = slice(g * 8, g * 8 + 8)
        second, third = coarse_shares({x: work_coarse[pl.ds(g * 128 + x, 8, stride=16), :] for x in range(NB)})
        for x in range(8):
            own_coarse[x, rows] = jnp.where(lanes.second, second[x], third[x // 2]) if x % 2 == 0 else second[x]
        near_low, near_high, far_low, far_high = send_rows(second, third, lanes)
        for i in range(4):
            to_low[320 + i * 40 + g * 8 : 320 + i * 40 + g * 8 + 8] = near_low[i]
            to_high[240 + i * 40 + g * 8 : 240 + i * 40 + g * 8 + 8] = near_high[i]
        to_low_far[rows] = far_low
        to_high_far[rows] = far_high


def tiles_kernel(targets, fine, from_high, from_low, tiles, outbox):
    outbox[...] = jnp.zeros_like(outbox)
    for g in range(10):
        rows = slice(g * 8, g * 8 + 8)
        for x in range(NB):
            row = fine[x, rows]
            if x < 3:
                row = row + from_low[x * 80 + g * 8 : x * 80 + g * 8 + 8]
            if x >= 12:
                i = x - 12
                row = row + from_high[i * 80 + g * 8 : i * 80 + g * 8 + 8]
            tiles[pl.ds(g * 128 + x, 8, stride=16), :] = row
    for t in range(1, TILES, 2):
        to = pl.multiple_of(targets[t] * 16, 16)
        outbox[pl.ds(to, 16), :] = tiles[t * 16 : t * 16 + 16]


def route_kernel(
    targets, tiles, coarse, from_high, from_low, from_high_far, from_low_far, filled,
    outbox, filling, low_rows, spread, sems,
):
    del filled
    shape = (8, LN)
    lanes = Lanes()
    even_row = lax.broadcasted_iota(jnp.int32, shape, 0) % 2 == 0
    replaced = (lanes.lane % 4 == 0) & even_row
    merged = lanes.second & even_row
    for g in range(5):
        rows = slice(g * 8, g * 8 + 8)
        added = add_coarse(
            [coarse[x, rows] for x in range(8)],
            [from_high[320 + i * 40 + g * 8 : 320 + i * 40 + g * 8 + 8] for i in range(4)],
            [from_low[240 + i * 40 + g * 8 : 240 + i * 40 + g * 8 + 8] for i in range(4)],
            from_high_far[rows],
            from_low_far[rows],
            lanes,
        )
        for x in range(8):
            row = added[x]
            if x % 2 == 0:
                row = jnp.where(replaced, lanes.roll(row, -1), row)
            for odd in range(2):
                spread[pl.ds(g * 128 + 2 * x + odd, 8, stride=16), :] = row
        for z in range(0, NB, 2):
            t = g * NB + z
            to = pl.multiple_of(targets[t] * 16, 16)
            for half in (0, 8):
                at = (g * 8 + z // 2) * 16 + half
                row = jnp.where(merged, spread[at : at + 8], tiles[t * 16 + half : t * 16 + half + 8])
                filling[pl.ds(to + half, 8), :] = row
        low_rows[g * 8 : g * 8 + 8] = added[0]
        low_rows[40 + g * 8 : 40 + g * 8 + 8] = added[4]
    copies = []
    for i in range(16):
        rows = pl.ds(i * 128, 128)
        copies.append(pltpu.make_async_copy(filling.at[rows], outbox.at[rows], sems.at[i]))
    for copy in copies:
        copy.start()
    for copy in copies:
        copy.wait()


def pick_kernel(rows, low_band):
    picked = (LN, 16)
    pick = lax.broadcasted_iota(jnp.int32, picked, 0) == 8 * lax.broadcasted_iota(jnp.int32, picked, 1) + 1
    pick = jnp.where(pick, jnp.ones(picked, jnp.float32), jnp.zeros(picked, jnp.float32)).astype(jnp.bfloat16)
    upper, lower = halves(rows[...])
    rest = (rows[...] - upper.astype(jnp.float32) - lower.astype(jnp.float32)).astype(jnp.bfloat16)
    dims = ((1,), (0,))
    low_band[...] = dot(upper, pick, dims) + dot(lower, pick, dims) + dot(rest, pick, dims)


VM = pl.BlockSpec(memory_space=pltpu.VMEM)
SM = pl.BlockSpec(memory_space=pltpu.SMEM)
HB = pl.BlockSpec(memory_space=pltpu.HBM)


def f32(*shape):
    return jax.ShapeDtypeStruct(shape, jnp.float32)


def call(kernel, outs, ins, scratch=(), specs=None, out_specs=None, flops=1 << 20, grant=32 << 20, aliases=None):
    moved = sum(4 * int(np.prod(a.shape)) for a in list(outs) + list(ins))
    return pl.pallas_call(
        kernel,
        out_shape=list(outs),
        in_specs=specs or [VM] * len(ins),
        out_specs=out_specs or [VM] * len(outs),
        scratch_shapes=list(scratch),
        input_output_aliases=aliases or {},
        compiler_params=pltpu.CompilerParams(vmem_limit_bytes=grant),
        cost_estimate=pl.CostEstimate(flops=flops, bytes_accessed=moved, transcendentals=0),
    )(*ins)


def shift(array, axis, by):
    count = lax.axis_size(axis)
    return lax.ppermute(array, axis, [(i, (i + by) % count) for i in range(count)])


def coarse_matrix(length):
    level_four = lift_np(np.eye(length))
    level_five = lift_np(level_four[0::2])
    level_four[0::2] = level_five
    return level_four.astype(np.float32)


def body(fields, tile_writer):
    send, own, place = y_matrices()
    send = jnp.asarray(np.concatenate(split(send)))
    maps = jnp.asarray(np.concatenate([*split(own), place.astype(ml_dtypes.bfloat16)]))
    cells = fields.reshape(ROWS, LN)
    writers = tile_writer.reshape(1, TILES)

    to_low, to_high, cells, maps, writers = call(
        share_y_kernel,
        [f32(16, ROWS), f32(16, ROWS), f32(ROWS, LN)] + [jax.ShapeDtypeStruct(a.shape, a.dtype) for a in (maps, writers)],
        [pltpu.with_memory_space_constraint(a, pltpu.HBM) for a in (cells, send, maps, writers)],
        [pltpu.VMEM((64, LN), jnp.bfloat16), pltpu.SemaphoreType.DMA((F + 3,))],
        [HB, HB, HB, HB],
        grant=32 << 20,
    )
    own, targets = call(
        own_y_kernel,
        [f32(ROWS, 2 * LN), jax.ShapeDtypeStruct((1, TILES), jnp.int32)],
        [writers, cells, maps],
        flops=1 << 30,
    )
    from_high = shift(to_low, "gy", -1)
    from_low = shift(to_high, "gy", 1)

    fine, coarse, to_low, to_high, to_low_far, to_high_far = call(
        share_z_kernel,
        [f32(ROWS, LN), f32(ROWS // 2, LN), f32(F, 8, 16, LN), f32(F, 7, 16, LN), f32(F, 16, LN), f32(F, 16, LN)],
        [own, maps, from_low, from_high],
        [pltpu.VMEM((ROWS, 2 * LN), jnp.float32)],
    )
    from_high = shift(to_low, "gz", -1)
    from_low = shift(to_high, "gz", 1)
    from_high_far = shift(to_low_far, "gz", -2)
    from_low_far = shift(to_high_far, "gz", 2)

    fine, to_low, to_high = call(
        fine_x_kernel,
        [f32(16, 80, LN), f32(480, LN), f32(400, LN)],
        [fine, from_high, from_low],
        [pltpu.VMEM((ROWS, LN), jnp.float32)],
        flops=1 << 30,
    )
    coarse, to_low, to_high, to_low_far, to_high_far = call(
        coarse_x_kernel,
        [f32(8, 40, LN), f32(480, LN), f32(400, LN), f32(40, LN), f32(40, LN)],
        [coarse, from_high, from_low, from_high_far, from_low_far, to_low, to_high],
        [pltpu.VMEM((ROWS // 2, LN), jnp.float32)],
        aliases={5: 1, 6: 2},
    )
    from_high = shift(to_low, "gx", -1)
    from_low = shift(to_high, "gx", 1)
    from_high_far = shift(to_low_far, "gx", -2)
    from_low_far = shift(to_high_far, "gx", 2)

    targets = targets.reshape(TILES)
    tiles, filling = call(
        tiles_kernel,
        [f32(ROWS, LN), f32(2048, LN)],
        [targets, fine, from_high, from_low],
        specs=[SM, VM, VM, VM],
        flops=1 << 30,
    )
    outbox, _, low_rows = call(
        route_kernel,
        [f32(2048, LN), f32(2048, LN), f32(80, LN)],
        [targets, tiles, coarse, from_high, from_low, from_high_far, from_low_far, filling],
        [pltpu.VMEM((640, LN), jnp.float32), pltpu.SemaphoreType.DMA((16,))],
        [SM] + [VM] * 7,
        [HB, VM, VM],
        aliases={7: 1},
    )
    inbox = lax.all_to_all(outbox.reshape(64, 32, LN), ("gx", "gy"), split_axis=0, concat_axis=0, tiled=True)

    (low_band,) = call(pick_kernel, [f32(80, 16)], [low_rows])
    band = low_band.reshape(2, F, 8, 16)[:, :, ::4].transpose(2, 1, 0, 3).reshape(2, F * 32)
    band = lax.all_gather(band, "gz", axis=0, tiled=True)
    turn = jnp.asarray(coarse_matrix(band.shape[0]))
    bands = jnp.dot(turn, band, precision=lax.Precision.HIGHEST)
    bands = bands.reshape(-1, F, 2, 16).transpose(1, 0, 2, 3)
    return (bands, inbox.reshape(128, 2048))


def solution(mesh):
    return jax.shard_map(
        body,
        mesh=mesh,
        in_specs=(P(None, "gz", "gx", "gy"), P("gx", "gy", "gz", None)),
        out_specs=(P(None, None, "gx", "gy"), P(("gx", "gy"), "gz")),
        check_vma=False,
    )
```

```python
import jax
import jax.numpy as jnp
import ml_dtypes
import numpy as np
from jax import lax
from jax.experimental import pallas as pl
from jax.experimental.pallas import tpu as pltpu
from jax.sharding import PartitionSpec as P

PREDICT_ONE = -1.586134342059924
UPDATE_ONE = -0.052980118572961
PREDICT_TWO = 0.882911075530934
UPDATE_TWO = 0.443506852043971
LOW_SCALE = 1.0 / 1.149604398860241
HIGH_SCALE = 1.149604398860241

F = 5
NB = 16
LN = 128
ROWS = F * NB * NB
TILES = F * NB

LOW_SIDE = (4, 6, 6)
HIGH_SIDE = (3, 5, 7)


def lift_np(values):
    low = values[0::2].copy()
    high = values[1::2].copy()
    high += PREDICT_ONE * (low + np.roll(low, -1, 0))
    low += UPDATE_ONE * (np.roll(high, 1, 0) + high)
    high += PREDICT_TWO * (low + np.roll(low, -1, 0))
    low += UPDATE_TWO * (np.roll(high, 1, 0) + high)
    joined = np.empty_like(values)
    joined[0::2] = low * LOW_SCALE
    joined[1::2] = high * HIGH_SCALE
    return joined


def split(matrix):
    matrix = np.asarray(matrix, np.float32)
    upper = matrix.astype(ml_dtypes.bfloat16)
    lower = (matrix - upper.astype(np.float32)).astype(ml_dtypes.bfloat16)
    return upper, lower


def y_matrices():
    total, start = 8 * LN, 4 * LN
    level = np.eye(total)
    maps = []
    for _ in range(3):
        level = lift_np(level)
        maps.append(level)
        level = level[0::2]
    own = np.zeros((LN, 2 * LN))
    send = np.zeros((32, LN))
    place = np.zeros((32, 2 * LN))
    columns = [lambda j: j, lambda j: LN + 2 * j, lambda j: LN + 4 * j + 1]
    at_low, at_high = 0, 16
    for depth in range(3):
        count = LN >> depth
        first = start >> depth
        block = maps[depth][:, start : start + LN]
        low, high = LOW_SIDE[depth], HIGH_SIDE[depth]
        assert not block[: first - low].any() and not block[first + count + high :].any()
        for j in range(count):
            own[:, columns[depth](j)] = block[first + j]
        for j in range(low):
            send[at_low] = block[first - low + j]
            place[at_low, columns[depth](count - low + j)] = 1
            at_low += 1
        for j in range(high):
            send[at_high] = block[first + count + j]
            place[at_high, columns[depth](j)] = 1
            at_high += 1
    return send, own, place


def lift(values):
    low = {i // 2: v for i, v in values.items() if i % 2 == 0}
    high = {i // 2: v for i, v in values.items() if i % 2 != 0}

    def add(target, source, factor, offsets):
        span = range(min(source) - 1, max(source) + 2)
        result = dict(target)
        for i in span:
            terms = [source[i + o] for o in offsets if i + o in source]
            if terms:
                step = factor * (terms[0] + terms[1] if len(terms) == 2 else terms[0])
                result[i] = result[i] + step if i in result else step
        return result

    high = add(high, low, PREDICT_ONE, (0, 1))
    low = add(low, high, UPDATE_ONE, (-1, 0))
    high = add(high, low, PREDICT_TWO, (0, 1))
    low = add(low, high, UPDATE_TWO, (-1, 0))
    joined = {2 * i: v * LOW_SCALE for i, v in low.items()}
    joined.update({2 * i + 1: v * HIGH_SCALE for i, v in high.items()})
    return joined


def lows(values):
    return {i // 2: v for i, v in values.items() if i % 2 == 0}


def dot(a, b, dims):
    return lax.dot_general(a, b, (dims, ((), ())), preferred_element_type=jnp.float32)


def halves(x):
    upper = x.astype(jnp.bfloat16)
    return upper, (x - upper.astype(jnp.float32)).astype(jnp.bfloat16)


def share_y_kernel(fields, send, maps, writers, to_low, to_high, cells, held, held_writers, matrix, sems):
    copies = [pltpu.make_async_copy(send, matrix, sems.at[F])]
    for f in range(F):
        rows = pl.ds(f * 256, 256)
        copies.append(pltpu.make_async_copy(fields.at[rows], cells.at[rows], sems.at[f]))
    copies.append(pltpu.make_async_copy(maps, held, sems.at[F + 1]))
    copies.append(pltpu.make_async_copy(writers, held_writers, sems.at[F + 2]))
    for copy in copies:
        copy.start()
    copies[0].wait()
    both, send_hi = matrix[...], matrix[:32]
    dims = ((1,), (1,))
    for f in range(F):
        rows = slice(f * 256, f * 256 + 256)
        copies[1 + f].wait()
        cells_hi, cells_lo = halves(cells[rows])
        upper = dot(both, cells_hi, dims)
        shares = upper[:32] + dot(send_hi, cells_lo, dims) + upper[32:]
        to_low[:, rows] = shares[:16]
        to_high[:, rows] = shares[16:]
    copies[F + 1].wait()
    copies[F + 2].wait()


def fine_shares(values):
    return lift(values)


def coarse_shares(values):
    second = lift(lows(lift(values)))
    third = lift(lows(second))
    return second, third


class Lanes:
    def __init__(self):
        self.lane = lax.broadcasted_iota(jnp.int32, (8, LN), 1)
        self.second = self.lane % 2 == 0
        self.third = self.lane % 4 == 1
        self.ahead = [self.lane % 4 == (1 + i) % 4 for i in range(4)]

    @staticmethod
    def roll(x, by):
        return pltpu.roll(x, by % LN, 1) if by % LN else x

    def pack_second(self, rows):
        packed = []
        for i in range(0, len(rows), 2):
            odd = self.roll(rows[i + 1], 1) if i + 1 < len(rows) else rows[i]
            packed.append(jnp.where(self.second, rows[i], odd))
        return packed

    def pack_third(self, rows):
        packed = rows[0]
        for i in range(1, len(rows)):
            packed = jnp.where(self.ahead[i], self.roll(rows[i], i), packed)
        return packed


def send_rows(second, third, lanes):
    near_low = lanes.pack_second([second[i - 6] for i in range(6)]) + [lanes.pack_third([third[i - 4] for i in range(4)])]
    near_high = lanes.pack_second([second[8 + i] for i in range(5)]) + [lanes.pack_third([third[4 + i] for i in range(4)])]
    return near_low, near_high, lanes.pack_third([third[-6], third[-5]]), lanes.pack_third([third[8], third[9], third[10]])


def slots_of(row):
    shape = (TILES, TILES)
    wide = jnp.broadcast_to(row, shape)
    other = lax.broadcasted_iota(jnp.int32, shape, 0)
    tile = lax.broadcasted_iota(jnp.int32, shape, 1)
    zero = jnp.zeros(shape, jnp.float32)
    column = jnp.sum(jnp.where(other == tile, wide, zero), axis=1, keepdims=True)
    equal = jnp.where((wide == column) & (other < tile), zero + 1, zero)
    return row * 2 + jnp.sum(equal, axis=0, keepdims=True)


def own_y_kernel(writers, fields, maps, own, targets):
    cells_hi, cells_lo = halves(fields[...])
    dims = ((1,), (0,))
    own_hi, own_lo = maps[:128], maps[128:256]
    own[...] = dot(cells_hi, own_hi, dims) + dot(cells_lo, own_hi, dims) + dot(cells_hi, own_lo, dims)
    targets[...] = slots_of(writers[...].astype(jnp.float32)).astype(jnp.int32)


def share_z_kernel(
    own, maps, from_low, from_high, fine, coarse, to_low, to_high, to_low_far, to_high_far, work
):
    shares = halves(jnp.concatenate([from_high[...], from_low[...]]))
    place = maps[256:]
    turned = ((0,), (0,))
    work[...] = own[...] + dot(jnp.concatenate(shares), jnp.concatenate([place, place]), turned)
    lanes = Lanes()
    for f in range(F):
        for half in (0, 8):
            rows = slice(half, half + 8)
            at = [f * 256 + z * 16 + half for z in range(NB)]
            done = fine_shares({z: work[at[z] : at[z] + 8, :LN] for z in range(NB)})
            for z in range(NB):
                fine[at[z] : at[z] + 8] = done[z]
            for i in range(4):
                to_low[f, i, rows] = done[i - 4]
            for i in range(3):
                to_high[f, i, rows] = done[16 + i]
            second, third = coarse_shares({z: work[at[z] : at[z] + 8, LN:] for z in range(NB)})
            for z in range(8):
                row = jnp.where(lanes.second, second[z], third[z // 2]) if z % 2 == 0 else second[z]
                coarse[f * 128 + z * 16 + half : f * 128 + z * 16 + half + 8] = row
            near_low, near_high, far_low, far_high = send_rows(second, third, lanes)
            for i in range(4):
                to_low[f, 4 + i, rows] = near_low[i]
                to_high[f, 3 + i, rows] = near_high[i]
            to_low_far[f, rows] = far_low
            to_high_far[f, rows] = far_high


def add_coarse(base, near_low, near_high, far_low, far_high, lanes):
    zero = jnp.zeros_like(base[0])
    extra = [zero] * 8
    for i in range(6):
        extra[2 + i] = extra[2 + i] + lanes.roll(near_low[i // 2], -(i % 2))
    for i in range(5):
        extra[i] = extra[i] + lanes.roll(near_high[i // 2], -(i % 2))
    near = near_low[3] + near_high[3]
    near = near + jnp.where(lanes.ahead[3], zero, far_high)
    third = [lanes.roll(near, -r) for r in range(4)]
    third[2] = third[2] + far_low
    third[3] = third[3] + lanes.roll(far_low, -1)
    rows = []
    for i in range(8):
        other = jnp.where(lanes.third, third[i // 2], zero) if i % 2 == 0 else zero
        rows.append(base[i] + jnp.where(lanes.second, extra[i], other))
    return rows


def fine_x_kernel(fine, from_high, from_low, own_fine, to_low, to_high, work):
    for f in range(F):
        at = f * 256
        work[at : at + 48] = fine[at : at + 48] + from_low[f, :3].reshape(48, LN)
        work[at + 48 : at + 192] = fine[at + 48 : at + 192]
        work[at + 192 : at + 256] = fine[at + 192 : at + 256] + from_high[f, :4].reshape(64, LN)
    for g in range(10):
        rows = slice(g * 8, g * 8 + 8)
        done = fine_shares({x: work[pl.ds(g * 128 + x, 8, stride=16), :] for x in range(NB)})
        for x in range(NB):
            own_fine[x, rows] = done[x]
        for i in range(4):
            to_low[i * 80 + g * 8 : i * 80 + g * 8 + 8] = done[i - 4]
        for i in range(3):
            to_high[i * 80 + g * 8 : i * 80 + g * 8 + 8] = done[16 + i]


def coarse_x_kernel(
    coarse, from_high, from_low, from_high_far, from_low_far, held_low, held_high,
    own_coarse, to_low, to_high, to_low_far, to_high_far, work_coarse,
):
    del held_low, held_high
    lanes = Lanes()
    for f in range(F):
        for half in (0, 8):
            rows = slice(half, half + 8)
            at = [f * 128 + z * 16 + half for z in range(8)]
            added = add_coarse(
                [coarse[at[z] : at[z] + 8] for z in range(8)],
                [from_high[f, 4 + i, rows] for i in range(4)],
                [from_low[f, 3 + i, rows] for i in range(4)],
                from_high_far[f, rows],
                from_low_far[f, rows],
                lanes,
            )
            for z in range(8):
                work_coarse[at[z] : at[z] + 8] = added[z]
    for g in range(5):
        rows = slice(g * 8, g * 8 + 8)
        second, third = coarse_shares({x: work_coarse[pl.ds(g * 128 + x, 8, stride=16), :] for x in range(NB)})
        for x in range(8):
            own_coarse[x, rows] = jnp.where(lanes.second, second[x], third[x // 2]) if x % 2 == 0 else second[x]
        near_low, near_high, far_low, far_high = send_rows(second, third, lanes)
        for i in range(4):
            to_low[320 + i * 40 + g * 8 : 320 + i * 40 + g * 8 + 8] = near_low[i]
            to_high[240 + i * 40 + g * 8 : 240 + i * 40 + g * 8 + 8] = near_high[i]
        to_low_far[rows] = far_low
        to_high_far[rows] = far_high


def tiles_kernel(targets, fine, from_high, from_low, tiles, outbox):
    outbox[...] = jnp.zeros_like(outbox)
    for g in range(10):
        rows = slice(g * 8, g * 8 + 8)
        for x in range(NB):
            row = fine[x, rows]
            if x < 3:
                row = row + from_low[x * 80 + g * 8 : x * 80 + g * 8 + 8]
            if x >= 12:
                i = x - 12
                row = row + from_high[i * 80 + g * 8 : i * 80 + g * 8 + 8]
            tiles[pl.ds(g * 128 + x, 8, stride=16), :] = row
    for t in range(1, TILES, 2):
        to = pl.multiple_of(targets[t] * 16, 16)
        outbox[pl.ds(to, 16), :] = tiles[t * 16 : t * 16 + 16]


def route_kernel(
    targets, tiles, coarse, from_high, from_low, from_high_far, from_low_far, filled,
    outbox, filling, low_rows, spread, sems,
):
    del filled
    shape = (8, LN)
    lanes = Lanes()
    even_row = lax.broadcasted_iota(jnp.int32, shape, 0) % 2 == 0
    replaced = (lanes.lane % 4 == 0) & even_row
    merged = lanes.second & even_row
    for g in range(5):
        rows = slice(g * 8, g * 8 + 8)
        added = add_coarse(
            [coarse[x, rows] for x in range(8)],
            [from_high[320 + i * 40 + g * 8 : 320 + i * 40 + g * 8 + 8] for i in range(4)],
            [from_low[240 + i * 40 + g * 8 : 240 + i * 40 + g * 8 + 8] for i in range(4)],
            from_high_far[rows],
            from_low_far[rows],
            lanes,
        )
        for x in range(8):
            row = added[x]
            if x % 2 == 0:
                row = jnp.where(replaced, lanes.roll(row, -1), row)
            for odd in range(2):
                spread[pl.ds(g * 128 + 2 * x + odd, 8, stride=16), :] = row
        for z in range(0, NB, 2):
            t = g * NB + z
            to = pl.multiple_of(targets[t] * 16, 16)
            for half in (0, 8):
                at = (g * 8 + z // 2) * 16 + half
                row = jnp.where(merged, spread[at : at + 8], tiles[t * 16 + half : t * 16 + half + 8])
                filling[pl.ds(to + half, 8), :] = row
        low_rows[g * 8 : g * 8 + 8] = added[0]
        low_rows[40 + g * 8 : 40 + g * 8 + 8] = added[4]
    copies = []
    for i in range(4):
        rows = pl.ds(i * 512, 512)
        copies.append(pltpu.make_async_copy(filling.at[rows], outbox.at[rows], sems.at[i]))
    for copy in copies:
        copy.start()
    for copy in copies:
        copy.wait()


def pick_kernel(rows, low_band):
    picked = (LN, 16)
    pick = lax.broadcasted_iota(jnp.int32, picked, 0) == 8 * lax.broadcasted_iota(jnp.int32, picked, 1) + 1
    pick = jnp.where(pick, jnp.ones(picked, jnp.float32), jnp.zeros(picked, jnp.float32)).astype(jnp.bfloat16)
    upper, lower = halves(rows[...])
    rest = (rows[...] - upper.astype(jnp.float32) - lower.astype(jnp.float32)).astype(jnp.bfloat16)
    dims = ((1,), (0,))
    low_band[...] = dot(upper, pick, dims) + dot(lower, pick, dims) + dot(rest, pick, dims)


VM = pl.BlockSpec(memory_space=pltpu.VMEM)
SM = pl.BlockSpec(memory_space=pltpu.SMEM)
HB = pl.BlockSpec(memory_space=pltpu.HBM)


def f32(*shape):
    return jax.ShapeDtypeStruct(shape, jnp.float32)


def call(kernel, outs, ins, scratch=(), specs=None, out_specs=None, flops=1 << 20, grant=32 << 20, aliases=None):
    moved = sum(4 * int(np.prod(a.shape)) for a in list(outs) + list(ins))
    return pl.pallas_call(
        kernel,
        out_shape=list(outs),
        in_specs=specs or [VM] * len(ins),
        out_specs=out_specs or [VM] * len(outs),
        scratch_shapes=list(scratch),
        input_output_aliases=aliases or {},
        compiler_params=pltpu.CompilerParams(vmem_limit_bytes=grant),
        cost_estimate=pl.CostEstimate(flops=flops, bytes_accessed=moved, transcendentals=0),
    )(*ins)


def shift(array, axis, by):
    count = lax.axis_size(axis)
    return lax.ppermute(array, axis, [(i, (i + by) % count) for i in range(count)])


def coarse_matrix(length):
    level_four = lift_np(np.eye(length))
    level_five = lift_np(level_four[0::2])
    level_four[0::2] = level_five
    return level_four.astype(np.float32)


def body(fields, tile_writer):
    send, own, place = y_matrices()
    send = jnp.asarray(np.concatenate(split(send)))
    maps = jnp.asarray(np.concatenate([*split(own), place.astype(ml_dtypes.bfloat16)]))
    cells = fields.reshape(ROWS, LN)
    writers = tile_writer.reshape(1, TILES)

    to_low, to_high, cells, maps, writers = call(
        share_y_kernel,
        [f32(16, ROWS), f32(16, ROWS), f32(ROWS, LN)] + [jax.ShapeDtypeStruct(a.shape, a.dtype) for a in (maps, writers)],
        [pltpu.with_memory_space_constraint(a, pltpu.HBM) for a in (cells, send, maps, writers)],
        [pltpu.VMEM((64, LN), jnp.bfloat16), pltpu.SemaphoreType.DMA((F + 3,))],
        [HB, HB, HB, HB],
        grant=32 << 20,
    )
    own, targets = call(
        own_y_kernel,
        [f32(ROWS, 2 * LN), jax.ShapeDtypeStruct((1, TILES), jnp.int32)],
        [writers, cells, maps],
        flops=1 << 30,
    )
    from_high = shift(to_low, "gy", -1)
    from_low = shift(to_high, "gy", 1)

    fine, coarse, to_low, to_high, to_low_far, to_high_far = call(
        share_z_kernel,
        [f32(ROWS, LN), f32(ROWS // 2, LN), f32(F, 8, 16, LN), f32(F, 7, 16, LN), f32(F, 16, LN), f32(F, 16, LN)],
        [own, maps, from_low, from_high],
        [pltpu.VMEM((ROWS, 2 * LN), jnp.float32)],
    )
    from_high = shift(to_low, "gz", -1)
    from_low = shift(to_high, "gz", 1)
    from_high_far = shift(to_low_far, "gz", -2)
    from_low_far = shift(to_high_far, "gz", 2)

    fine, to_low, to_high = call(
        fine_x_kernel,
        [f32(16, 80, LN), f32(480, LN), f32(400, LN)],
        [fine, from_high, from_low],
        [pltpu.VMEM((ROWS, LN), jnp.float32)],
        flops=1 << 30,
    )
    coarse, to_low, to_high, to_low_far, to_high_far = call(
        coarse_x_kernel,
        [f32(8, 40, LN), f32(480, LN), f32(400, LN), f32(40, LN), f32(40, LN)],
        [coarse, from_high, from_low, from_high_far, from_low_far, to_low, to_high],
        [pltpu.VMEM((ROWS // 2, LN), jnp.float32)],
        aliases={5: 1, 6: 2},
    )
    from_high = shift(to_low, "gx", -1)
    from_low = shift(to_high, "gx", 1)
    from_high_far = shift(to_low_far, "gx", -2)
    from_low_far = shift(to_high_far, "gx", 2)

    targets = targets.reshape(TILES)
    tiles, filling = call(
        tiles_kernel,
        [f32(ROWS, LN), f32(2048, LN)],
        [targets, fine, from_high, from_low],
        specs=[SM, VM, VM, VM],
        flops=1 << 30,
    )
    outbox, _, low_rows = call(
        route_kernel,
        [f32(2048, LN), f32(2048, LN), f32(80, LN)],
        [targets, tiles, coarse, from_high, from_low, from_high_far, from_low_far, filling],
        [pltpu.VMEM((640, LN), jnp.float32), pltpu.SemaphoreType.DMA((4,))],
        [SM] + [VM] * 7,
        [HB, VM, VM],
        aliases={7: 1},
    )
    inbox = lax.all_to_all(outbox.reshape(64, 32, LN), ("gx", "gy"), split_axis=0, concat_axis=0, tiled=True)

    (low_band,) = call(pick_kernel, [f32(80, 16)], [low_rows])
    band = low_band.reshape(2, F, 8, 16)[:, :, ::4].transpose(2, 1, 0, 3).reshape(2, F * 32)
    band = lax.all_gather(band, "gz", axis=0, tiled=True)
    turn = jnp.asarray(coarse_matrix(band.shape[0]))
    bands = jnp.dot(turn, band, precision=lax.Precision.HIGHEST)
    bands = bands.reshape(-1, F, 2, 16).transpose(1, 0, 2, 3)
    return (bands, inbox.reshape(128, 2048))


def solution(mesh):
    return jax.shard_map(
        body,
        mesh=mesh,
        in_specs=(P(None, "gz", "gx", "gy"), P("gx", "gy", "gz", None)),
        out_specs=(P(None, None, "gx", "gy"), P(("gx", "gy"), "gz")),
        check_vma=False,
    )
```
